512 devices in a mesh: gx: 4 (over x), gy: 16 (over z, core), gz: 8 (over y).
Axes of the slice: x: 4, y: 8, z: 8, core: 2. Of those that a mesh axis runs over, the one named last changes fastest.
Arguments:
- velocity_partial: float32 [3, 32, 256, 1024], P(None, 'gx', 'gy', 'gz'), may hold values from -6 to 6
- pressure_source: float32 [32, 256, 1024], P('gx', 'gy', 'gz'), may hold values from -6 to 6
- metric: float32 [3, 32, 256, 1024], P(None, 'gx', 'gy', 'gz'), may hold values from 0.02 to 0.2
- screening: float32 [32, 256, 1024], P('gx', 'gy', 'gz'), may hold values from 0.5 to 5
- particle_coords: float32 [3, 262144], P(None, ('gx', 'gy', 'gz')), may hold values from -1 to 1
- particle_owner: int32 [262144, 1], P(('gx', 'gy', 'gz')), may hold values from 0 to 15; in each aligned block of 512 rows (0 to 511, 512 to 1023, ...) at most 128 rows name the same one
- particle_element: int32 [262144], P(('gx', 'gy', 'gz')), may hold values from 0 to 31
Outputs:
- pressure: float32 [32, 256, 1024], P('gx', 'gy', 'gz')
- particle_velocity: float32 [3, 262144], P(None, ('gx', 'gy', 'gz'))
The draws below stay inside these ranges and needn't reach their ends.
Inputs may be any that keep to these rules, and one draw needn't show every extreme that they name: `particle_owner`: among the 512 particles of one device, at most 128 name the same owner, and on every device some owner is named by exactly 128.
All inputs are finite; a program needn't handle non-finite values.
Results may differ from the reference program's by a relative error of at most 0.0003.
Values sent between devices are 32-bit elements; how exact they have to be, the bound alone decides.
A program may use at most 128 MiB of HBM per device.

```python
import math
import jax
import jax.numpy as jnp
import numpy as np
from jax import lax

EX = 1
EY = 2
EZ = 16
ITERS = 3
P_DEV = 512
CAP = 128
E_DEV = 32
GXN = 32
GYN = 256
GZN = 1024
P_TOTAL = 262144
N_GY = 16
N_GZ = 8
DEVICES = 512


def with_ends(drawn, rng, low, high):
    longest = drawn.shape.index(max(drawn.shape))
    spots = []
    for shift in (0, 1):
        where = [jax.random.randint(jax.random.fold_in(rng, axis), (), 0, length) for axis, length in enumerate(drawn.shape)]
        where[longest] = (where[longest] + shift) % drawn.shape[longest]
        spots.append(tuple(where))
    return drawn.at[spots[0]].set(low).at[spots[1]].set(high)


def shard_levels(key, extent, split, low, top_value):
    factor_of, own = 1.0, jax.random.fold_in(key, 6)
    for dim, blocks in split:
        heights = jnp.exp(jax.random.uniform(jax.random.fold_in(own, dim), (blocks,), jnp.float32, low / len(split), top_value / len(split)))
        factor_of = factor_of * jnp.repeat(heights, extent[dim] // blocks).reshape([-1 if axis == dim else 1 for axis in range(len(extent))])
    return factor_of


def assign_block(rng, own, number, rows, number_of, top, bound, lean):
    sequence = jax.random.permutation(rng, number_of)
    packed, common = shares(number_of, rows * top, bound, lean, True), shares(number_of, rows * top, bound, lean, False)
    places = jnp.arange(number_of)

    def named(sizes, turn):
        used = int((sizes > 0).sum())
        fixed = max(1, used // 4)
        moved = fixed + (places - fixed + turn * (used - fixed)) % max(1, number_of - fixed)
        return jnp.zeros((number_of,), jnp.int32).at[sequence[jnp.where(places < fixed, places, moved)]].set(jnp.asarray(sizes, jnp.int32))

    sizes = jnp.where(number % 4 == 0, named(packed, number // 4), named(common, number - number // 4 - 1))
    mixed = jax.random.permutation(jax.random.fold_in(own, 3), number_of)
    giver, receiver = mixed[0:number_of // 2 * 2:2], mixed[1:number_of // 2 * 2:2]
    margin = jnp.minimum(sizes[giver] - 1, bound - sizes[receiver]) // 2
    margin = jnp.where((giver == sequence[0]) | (receiver == sequence[0]) | (sizes[receiver] == 0), 0, jnp.maximum(margin, 0))
    moved = jax.random.randint(jax.random.fold_in(own, 4), (number_of // 2,), 0, 1 << 20) % (margin + 1)
    sizes = sizes.at[giver].add(-moved).at[receiver].add(moved)
    members = jnp.searchsorted(jnp.cumsum(sizes), jnp.arange(rows * top), side="right").astype(jnp.int32)
    listing = members.reshape(top, rows).T
    listing = listing[jax.random.permutation(jax.random.fold_in(own, 1), rows)]
    turn = jax.random.randint(jax.random.fold_in(own, 2), (rows, 1), 0, top)
    return jnp.take_along_axis(listing, (jnp.arange(top)[None, :] + turn) % top, axis=1)


def shares(count, total, limit, lean, full):
    weights = [(1 << 20) // math.isqrt(rank ** lean) + 1 for rank in range(1, count + 1)]
    largest = limit if full else min(limit, max(-(-total // count), total * weights[0] // sum(weights)))
    least = 1 if total - largest >= count - 1 else 0
    counts, surplus = [largest] + [least] * (count - 1), total - largest - least * (count - 1)
    while surplus > 0:
        movable = [i for i in range(1, count) if counts[i] < largest] or [i for i in range(1, count) if counts[i] < limit]
        mass, budget = sum([weights[i] for i in movable]), surplus
        for i in movable:
            extra = min(limit - counts[i], max(1, budget * weights[i] // mass), surplus)
            counts[i] = counts[i] + extra
            surplus = surplus - extra
    return np.array(counts)


def centred(stream_key, shape, width, reach, cuts=(), held_as=jnp.bfloat16):
    factor_of = shard_levels(stream_key, shape, cuts, -0.22, 0.18) if cuts else 1.0
    entries = jax.random.normal(stream_key, shape, jnp.float32) * width * factor_of
    return jnp.minimum(jnp.maximum(entries, -reach), reach).astype(held_as)


def setup_inputs(seed: int = 0) -> dict:
    key_of = jax.random.split(jax.random.key(seed), 8)
    velocity_partial = centred(key_of[0], (3, GXN, GYN, GZN), 1.0, 6.0, ((1, 4), (2, 16), (3, 8)), jnp.float32)
    pressure_source = centred(key_of[1], (GXN, GYN, GZN), 1.0, 6.0, ((0, 4), (1, 16), (2, 8)), jnp.float32)
    metric = jnp.clip(jnp.exp(math.log(0.2) - 2.3025851 * jax.random.uniform(key_of[2], (3, GXN, GYN, GZN), jnp.float32) ** shard_levels(key_of[2], (3, GXN, GYN, GZN), ((1, 4), (2, 16), (3, 8)), -0.2, 0.2)), 0.02, 0.2)
    screening = jnp.clip(jnp.exp(math.log(5.0) - 2.3025851 * jax.random.uniform(key_of[3], (GXN, GYN, GZN), jnp.float32) ** shard_levels(key_of[3], (GXN, GYN, GZN), ((0, 4), (1, 16), (2, 8)), -0.2, 0.2)), 0.5, 5.0)
    particle_coords = jnp.clip(jax.random.uniform(key_of[4], (3, P_TOTAL), jnp.float32, -1.0, 1.0) * shard_levels(key_of[4], (3, P_TOTAL), ((1, 512),), -0.4, 0.0), -1.0, 1.0)
    particle_owner_keys = jax.random.split(jax.random.fold_in(key_of[5], 1), P_TOTAL // P_DEV)
    particle_owner_turns = jax.random.permutation(jax.random.fold_in(key_of[5], 3), P_TOTAL // P_DEV)
    particle_owner = jax.vmap(lambda own, number: assign_block(jax.random.fold_in(key_of[5], 2), own, number, P_DEV, N_GY, 1, CAP, 2))(particle_owner_keys, particle_owner_turns).reshape((P_TOTAL, 1))
    particle_element = with_ends(jax.random.randint(key_of[6], (P_TOTAL,), 0, E_DEV), jax.random.fold_in(key_of[6], 1), 0, E_DEV - 1).astype(jnp.int32)
    return dict(velocity_partial=velocity_partial, pressure_source=pressure_source, metric=metric, screening=screening, particle_coords=particle_coords, particle_owner=particle_owner, particle_element=particle_element)


def gll_points():
    return [-1.0, -0.8717401485096066, -0.5917001814331423, -0.2092992179024789,
            0.2092992179024789, 0.5917001814331423, 0.8717401485096066, 1.0]


def legendre_seven(point):
    before, current = 1.0, point
    for order in range(1, 7):
        before, current = current, ((2 * order + 1) * point * current - order * before) / (order + 1)
    return current


def deriv_table():
    points = gll_points()
    legendre = [legendre_seven(value) for value in points]
    derivative = [[0.0] * 8 for row in range(8)]
    for i in range(8):
        for j in range(8):
            if i != j:
                derivative[i][j] = legendre[i] / legendre[j] / (points[i] - points[j])
    derivative[0][0] = -14.0
    derivative[7][7] = 14.0
    return derivative


def pair_sum(padded, axis):
    length = padded.shape[axis] - 2
    center = lax.slice_in_dim(padded, 1, length + 1, axis=axis)
    lower_rows = lax.slice_in_dim(padded, 0, length, axis=axis)
    upper_rows = lax.slice_in_dim(padded, 2, length + 2, axis=axis)
    position = lax.broadcasted_iota(jnp.int32, center.shape, axis) % 8
    return center + jnp.where(position == 0, lower_rows, 0.0) + jnp.where(position == 7, upper_rows, 0.0)


def assemble_padded(padded):
    return pair_sum(pair_sum(pair_sum(padded, 1), 2), 3)


def pad_global(fields):
    padded = jnp.pad(fields, ((0, 0), (1, 1), (0, 0), (0, 0)), mode="wrap")
    padded = jnp.pad(padded, ((0, 0), (0, 0), (1, 1), (0, 0)))
    return jnp.pad(padded, ((0, 0), (0, 0), (0, 0), (1, 1)), mode="wrap")


def local_operator(field_in, metric, screening):
    extent_x, extent_y, extent_z = field_in.shape
    matrix = jnp.asarray(deriv_table(), dtype=jnp.float32)
    exact = lax.Precision.HIGHEST

    def along_x(values, table):
        shaped = values.reshape(extent_x // 8, 8, extent_y, extent_z)
        return jnp.einsum("ai,eiyz->eayz", table, shaped, precision=exact).reshape(extent_x, extent_y, extent_z)

    def along_y(values, table):
        shaped = values.reshape(extent_x, extent_y // 8, 8, extent_z)
        return jnp.einsum("ai,xeiz->xeaz", table, shaped, precision=exact).reshape(extent_x, extent_y, extent_z)

    def along_z(values, table):
        shaped = values.reshape(extent_x, extent_y, extent_z // 8, 8)
        return jnp.einsum("ai,xyei->xyea", table, shaped, precision=exact).reshape(extent_x, extent_y, extent_z)

    result = along_x(metric[0] * along_x(field_in, matrix), matrix.T)
    result = result + along_y(metric[1] * along_y(field_in, matrix), matrix.T)
    result = result + along_z(metric[2] * along_z(field_in, matrix), matrix.T)
    return result + screening * field_in


def share_weight(shape, y_start, y_total):
    x_place = lax.broadcasted_iota(jnp.int32, shape, 0) % 8
    x_share = jnp.where((x_place == 0) | (x_place == 7), 0.5, 1.0)
    y_global = lax.broadcasted_iota(jnp.int32, shape, 1) + y_start
    y_place = y_global % 8
    at_wall = (y_global == 0) | (y_global == y_total - 1)
    y_share = jnp.where(((y_place == 0) | (y_place == 7)) & jnp.logical_not(at_wall), 0.5, 1.0)
    z_place = lax.broadcasted_iota(jnp.int32, shape, 2) % 8
    z_share = jnp.where((z_place == 0) | (z_place == 7), 0.5, 1.0)
    return (x_share * y_share * z_share).astype(jnp.float32)


def lagrange_rows(coord):
    points = gll_points()
    basis_rows = []
    for i in range(8):
        factor = jnp.ones_like(coord)
        for m in range(8):
            if m != i:
                factor = factor * (coord - points[m]) / (points[i] - points[m])
        basis_rows.append(factor)
    return jnp.stack(basis_rows)


def sample(element_block, positions):
    exact = lax.Precision.HIGHEST
    basis_x = lagrange_rows(positions[0])
    basis_y = lagrange_rows(positions[1])
    basis_z = lagrange_rows(positions[2])
    partial_value = jnp.einsum("ncijk,kn->ncij", element_block, basis_z, precision=exact)
    partial_value = jnp.einsum("ncij,jn->nci", partial_value, basis_y, precision=exact)
    return jnp.einsum("nci,in->cn", partial_value, basis_x, precision=exact)


def reference(velocity_partial, pressure_source, metric, screening, particle_coords, particle_owner, particle_element):
    stacked = jnp.concatenate([velocity_partial, pressure_source[None]], axis=0)
    assembled = assemble_padded(pad_global(stacked))
    velocity = assembled[:3]
    residual = assembled[3]
    weight = share_weight(residual.shape, 0, residual.shape[1])

    def apply_operator(field_in):
        return assemble_padded(pad_global(local_operator(field_in, metric, screening)[None]))[0]

    pressure = jnp.zeros_like(residual)
    direction = residual
    norm_now = jnp.sum(weight * residual * residual)
    for iteration in range(ITERS):
        operator_image = apply_operator(direction)
        step_length = norm_now / jnp.sum(weight * direction * operator_image)
        pressure = pressure + step_length * direction
        residual = residual - step_length * operator_image
        norm_next = jnp.sum(weight * residual * residual)
        direction = residual + (norm_next / norm_now) * direction
        norm_now = norm_next

    extent_x, extent_y, extent_z = residual.shape
    element_table = velocity.reshape(3, extent_x // 8, 8, extent_y // 8, 8, extent_z // 8, 8).transpose(1, 3, 5, 0, 2, 4, 6)
    anchor = jnp.arange(P_TOTAL, dtype=jnp.int32) // P_DEV
    anchor_x = anchor // (N_GY * N_GZ)
    anchor_z = anchor % N_GZ
    owner_row = particle_owner[:, 0]
    local_x = particle_element // (EY * EZ)
    local_y = (particle_element // EZ) % EY
    local_z = particle_element % EZ
    global_x = (anchor_x * EX + local_x).reshape(DEVICES, P_DEV)
    global_y = (owner_row * EY + local_y).reshape(DEVICES, P_DEV)
    global_z = (anchor_z * EZ + local_z).reshape(DEVICES, P_DEV)
    positions = particle_coords.reshape(3, DEVICES, P_DEV).transpose(1, 0, 2)

    def sample_block(items):
        index_x, index_y, index_z, where_at = items
        return sample(element_table[index_x, index_y, index_z], where_at)

    values = lax.map(sample_block, (global_x, global_y, global_z, positions))
    particle_velocity = values.transpose(1, 0, 2).reshape(3, P_TOTAL)
    return pressure, particle_velocity
```

```python
import functools

import jax
import jax.numpy as jnp
import numpy as np
from jax import lax
from jax.experimental import pallas as pl
from jax.experimental.pallas import tpu as pltpu
from jax.sharding import PartitionSpec as P

MESH = pl.DeviceIdType.MESH
F32 = jnp.float32
BF16 = jnp.bfloat16
EXACT = lax.Precision.HIGHEST
SCALE = 1.0 / 64.0
GX, GY, GZ = 4, 16, 8
CAP = 128
FIELDS = 6


def gll_points():
    return [
        -1.0,
        -0.8717401485096066,
        -0.5917001814331423,
        -0.2092992179024789,
        0.2092992179024789,
        0.5917001814331423,
        0.8717401485096066,
        1.0,
    ]


def legendre_seven(point):
    before, current = (1.0, point)
    for order in range(1, 7):
        before, current = (
            current,
            ((2 * order + 1) * point * current - order * before) / (order + 1),
        )
    return current


def deriv_table():
    points = gll_points()
    legendre = [legendre_seven(value) for value in points]
    derivative = [[0.0] * 8 for row in range(8)]
    for i in range(8):
        for j in range(8):
            if i != j:
                derivative[i][j] = legendre[i] / legendre[j] / (points[i] - points[j])
    derivative[0][0] = -14.0
    derivative[7][7] = 14.0
    return derivative


def lagrange_scale():
    points = gll_points()
    scale = []
    for i in range(8):
        product = 1.0
        for m in range(8):
            if m != i:
                product *= points[i] - points[m]
        scale.append(1.0 / product)
    return scale


def iota(shape, dim):
    return lax.broadcasted_iota(jnp.int32, shape, dim)


def kernel(
    vel, src, met, scr, coords, owner, elem, ky, kyt, kz, kzt, lsc,
    p_out, pv_out,
    work, hxs, hx, hys, hyr, hzs, hzr, hss, hrs,
    msg, rx, rz, ry, ass, ars,
    sendp, recvp, sendv, recvv, pss, prs, vhi, vlo,
):
    gx, gy, gz = lax.axis_index("gx"), lax.axis_index("gy"), lax.axis_index("gz")

    def at_x(k):
        return (lax.rem(gx + (k + GX), GX), gy, gz)

    def at_y(k):
        return (gx, lax.rem(gy + (k + GY), GY), gz)

    def at_z(k):
        return (gx, gy, lax.rem(gz + (k + GZ), GZ))

    barrier = pltpu.get_barrier_semaphore()
    for k in range(1, GX):
        pl.semaphore_signal(barrier, inc=1, device_id=at_x(k), device_id_type=MESH)
    for k in range(1, GZ):
        pl.semaphore_signal(barrier, inc=1, device_id=at_z(k), device_id_type=MESH)
    for k in range(1, GY):
        pl.semaphore_signal(barrier, inc=1, device_id=at_y(k), device_id_type=MESH)

    sends = []

    def remote(src_ref, dst_ref, ssem, rsem, device):
        copy = pltpu.make_async_remote_copy(
            src_ref=src_ref,
            dst_ref=dst_ref,
            send_sem=ssem,
            recv_sem=rsem,
            device_id=device,
            device_id_type=MESH,
        )
        copy.start()
        sends.append(copy)
        return copy

    row_id = iota((128, 128), 0)
    lane_id = iota((128, 128), 1)
    eye = row_id == lane_id
    lane_in = lane_id % 8
    low_z = (lane_in == 0) & (lane_id > 0)
    high_z = (lane_in == 7) & (lane_id < 127)
    at_floor = gy == 0
    at_ceiling = gy == GY - 1

    def start_x(f, tail, head):
        return (
            remote(tail, hx.at[f, 0], hss.at[f, 0], hrs.at[f, 0], at_x(1)),
            remote(head, hx.at[f, 1], hss.at[f, 1], hrs.at[f, 1], at_x(-1)),
        )

    def start_image(f, field):
        work[f] = field
        hxs[f - 1, 0] = field[112:128, :]
        hxs[f - 1, 1] = field[0:16, :]
        return start_x(f, hxs.at[f - 1, 0], hxs.at[f - 1, 1])

    def mid_xy(f, copies):
        w = work.at[f]
        copies[0].wait_recv()
        w[pl.ds(0, 16), :] = w[pl.ds(0, 16), :] + hx[f, 0]
        copies[1].wait_recv()
        w[pl.ds(112, 16), :] = w[pl.ds(112, 16), :] + hx[f, 1]
        both = w[pl.ds(7, 8, stride=16), :] + w[pl.ds(8, 8, stride=16), :]
        w[pl.ds(7, 8, stride=16), :] = both
        w[pl.ds(8, 8, stride=16), :] = both
        hys[f, 0] = w[pl.ds(15, 8, stride=16), :]
        hys[f, 1] = w[pl.ds(0, 8, stride=16), :]
        return (
            remote(hys.at[f, 0], hyr.at[f, 0], hss.at[f, 2], hrs.at[f, 2], at_y(1)),
            remote(hys.at[f, 1], hyr.at[f, 1], hss.at[f, 3], hrs.at[f, 3], at_y(-1)),
        )

    def mid_yz(f, copies):
        w = work.at[f]
        copies[0].wait_recv()
        w[pl.ds(0, 8, stride=16), :] = w[pl.ds(0, 8, stride=16), :] + jnp.where(at_floor, 0.0, hyr[f, 0])
        copies[1].wait_recv()
        w[pl.ds(15, 8, stride=16), :] = w[pl.ds(15, 8, stride=16), :] + jnp.where(at_ceiling, 0.0, hyr[f, 1])
        field = w[...]
        hzs[f, 0] = jnp.sum(jnp.where(eye, field[:, 127:128], 0.0), axis=0, keepdims=True)
        hzs[f, 1] = jnp.sum(jnp.where(eye, field[:, 0:1], 0.0), axis=0, keepdims=True)
        out = (
            remote(hzs.at[f, 0], hzr.at[f, 0], hss.at[f, 4], hrs.at[f, 4], at_z(1)),
            remote(hzs.at[f, 1], hzr.at[f, 1], hss.at[f, 5], hrs.at[f, 5], at_z(-1)),
        )
        field = (
            field
            + jnp.where(low_z, pltpu.roll(field, 1, 1), 0.0)
            + jnp.where(high_z, pltpu.roll(field, 127, 1), 0.0)
        )
        return out, field

    def end_z(f, copies, field):
        copies[0].wait_recv()
        low = jnp.sum(jnp.where(eye, hzr[f, 0], 0.0), axis=1, keepdims=True)
        copies[1].wait_recv()
        high = jnp.sum(jnp.where(eye, hzr[f, 1], 0.0), axis=1, keepdims=True)
        return field + jnp.where(lane_id == 0, low, 0.0) + jnp.where(lane_id == 127, high, 0.0)

    table = deriv_table()

    def along_x(field, transposed):
        parts = [field[16 * i : 16 * i + 16, :] for i in range(8)]
        out = []
        for a in range(8):
            total = None
            for i in range(8):
                factor = table[i][a] if transposed else table[a][i]
                if factor == 0.0:
                    continue
                term = parts[i] * np.float32(factor)
                total = term if total is None else total + term
            out.append(total)
        return jnp.concatenate(out, axis=0)

    def gradients(field):
        return (
            along_x(field, False),
            jnp.dot(ky[...], field, precision=EXACT, preferred_element_type=F32),
            jnp.dot(field, kzt[...], precision=EXACT, preferred_element_type=F32),
        )

    def operator(field):
        dx, dy, dz = gradients(field)
        return (
            along_x(met[0] * dx, True)
            + jnp.dot(kyt[...], met[1] * dy, precision=EXACT, preferred_element_type=F32)
            + jnp.dot(met[2] * dz, kz[...], precision=EXACT, preferred_element_type=F32)
            + scr[...] * field
        ) * SCALE

    sendv[...] = jnp.zeros_like(sendv)
    work[0] = src[...]
    for c in range(3):
        work[3 + c] = vel[c]
    pl.semaphore_wait(barrier, (GX - 1) + (GY - 1) + (GZ - 1))

    cx = start_x(0, src.at[pl.ds(112, 16)], src.at[pl.ds(0, 16)])
    cv = [
        start_x(3 + c, vel.at[c, pl.ds(112, 16)], vel.at[c, pl.ds(0, 16)]) for c in range(3)
    ]

    owned = (owner[...] == iota((GY, 512), 0)).astype(F32)
    tri = (iota((128, 128), 0) < iota((128, 128), 1)).astype(BF16)
    before = jnp.zeros((GY, 1), F32)
    rank = []
    for b in range(4):
        part = owned[:, 128 * b : 128 * b + 128]
        count = jnp.dot(part.astype(BF16), tri, preferred_element_type=F32) + before
        rank.append(jnp.sum(count * part, axis=0, keepdims=True))
        before = before + jnp.sum(part, axis=1, keepdims=True)
    rank = jnp.concatenate(rank, axis=1)
    slots = (rank.astype(jnp.int32) == iota((CAP, 512), 0)).astype(F32)
    data = jnp.concatenate(
        [coords[...], elem[...].astype(F32), jnp.zeros((4, 512), F32)], axis=0
    )
    lhs = jnp.concatenate([data * owned[g : g + 1, :] for g in range(GY)], axis=0)
    packed = lax.dot_general(
        lhs, slots, (((1,), (1,)), ((), ())), precision=EXACT, preferred_element_type=F32
    )
    for g in range(GY):
        sendp[g] = packed[8 * g : 8 * g + 8, :]

    cy = mid_xy(0, cx)

    to_owner = []
    for k in range(1, GY):
        peer = lax.rem(gy + k, GY)
        to_owner.append(
            remote(sendp.at[peer], recvp.at[gy], pss.at[0, k], prs.at[0, k], (gx, peer, gz))
        )
    recvp[gy] = sendp[gy]

    czp, field = mid_yz(0, cy)
    cvy = []
    for c in range(3):
        cvy.append(mid_xy(3 + c, cv[c]))
    v0 = end_z(0, czp, field)

    cx = start_image(1, operator(v0))
    cvz = []
    vfield = []
    cy = mid_xy(1, cx)
    for c in range(3):
        out, value = mid_yz(3 + c, cvy[c])
        cvz.append(out)
        vfield.append(value)
    cz, field = mid_yz(1, cy)
    for c in range(3):
        value = end_z(3 + c, cvz[c], vfield[c])
        high = value.astype(BF16)
        vhi[pl.ds(128 * c, 128), :] = high
        vlo[pl.ds(128 * c, 128), :] = (value - high.astype(F32)).astype(BF16)
    v1 = end_z(1, cz, field)

    cx = start_image(2, operator(v1))

    for copy in to_owner:
        copy.wait_recv()
    points = gll_points()
    node = iota((8, 128), 0)

    def basis(coord):
        product = lsc[...]
        for m in range(8):
            product = product * jnp.where(node == m, 1.0, coord - np.float32(points[m]))
        return product

    def sample_two(step, carry):
        low_parts, high_parts, weights = [], [], []
        for half in range(2):
            block = recvp[2 * step + half]
            element = block[3:4, :].astype(jnp.int32)
            bx, by, bz = (basis(block[d : d + 1, :]) for d in range(3))
            element_y = element // 16
            element_z = element % 16
            wide = jnp.concatenate(
                [jnp.where(element_z == e, bz, 0.0) for e in range(16)], axis=0
            )
            high = wide.astype(BF16)
            high_parts.append(high)
            low_parts.append((wide - high.astype(F32)).astype(BF16))
            tall = jnp.concatenate(
                [jnp.where(element_y == e, by, 0.0) for e in range(2)], axis=0
            )
            weights.append(
                jnp.concatenate([bx[i : i + 1, :] * tall for i in range(8)], axis=0)
            )
        high = jnp.concatenate(high_parts, axis=1)
        low = jnp.concatenate(low_parts, axis=1)
        for c in range(3):
            vh = vhi[pl.ds(128 * c, 128), :]
            partial = (
                jnp.dot(vh, high, preferred_element_type=F32)
                + jnp.dot(vh, low, preferred_element_type=F32)
                + jnp.dot(vlo[pl.ds(128 * c, 128), :], high, preferred_element_type=F32)
            )
            for half in range(2):
                sendv[2 * step + half, pl.ds(c, 1), :] = jnp.sum(
                    partial[:, 128 * half : 128 * half + 128] * weights[half], axis=0, keepdims=True
                )
        return carry

    lax.fori_loop(0, GY // 2, sample_two, 0)

    cy = mid_xy(2, cx)
    to_home = []
    for k in range(1, GY):
        peer = lax.rem(gy + k, GY)
        to_home.append(
            remote(sendv.at[peer], recvv.at[gy], pss.at[1, k], prs.at[1, k], (gx, peer, gz))
        )
    recvv[gy] = sendv[gy]
    cz, field = mid_yz(2, cy)
    v2 = end_z(2, cz, field)

    place_y = row_id % 16
    share_x = jnp.where((row_id < 16) | (row_id >= 112), 0.5, 1.0)
    edge_y = (place_y % 8 == 0) | (place_y % 8 == 7)
    wall = ((place_y == 0) & at_floor) | ((place_y == 15) & at_ceiling)
    share_y = jnp.where(edge_y & jnp.logical_not(wall), 0.5, 1.0)
    share_z = jnp.where((lane_in == 0) | (lane_in == 7), 0.5, 1.0)
    weight = share_x * share_y * share_z
    dx, dy, dz = gradients(v2)
    products = [
        weight * v0 * v0,
        weight * v0 * v1,
        weight * v1 * v1,
        weight * v1 * v2,
        weight * v2 * v2,
        (met[0] * dx * dx + met[1] * dy * dy + met[2] * dz * dz + scr[...] * v2 * v2) * SCALE,
    ]
    rows = [jnp.sum(value, axis=0, keepdims=True) for value in products]
    rows = jnp.concatenate(rows + [jnp.zeros((2, 128), F32)], axis=0)
    total = jnp.sum(rows, axis=1, keepdims=True)
    row = jnp.sum(
        jnp.where(iota((8, 128), 0) == iota((8, 128), 1), total, 0.0), axis=0, keepdims=True
    )

    def reduce_over(stage, row, count, me, slots_ref, place, base):
        msg[stage] = row
        slots_ref[me] = row
        copies = [
            remote(msg.at[stage], slots_ref.at[me], ass.at[base + k], ars.at[base + k], place(k))
            for k in range(1, count)
        ]
        for copy in copies:
            copy.wait_recv()
        return jnp.sum(slots_ref[...], axis=0)

    row = reduce_over(0, row, GX, gx, rx, at_x, 0)
    row = reduce_over(1, row, GZ, gz, rz, at_z, GX)
    row = reduce_over(2, row, GY, gy, ry, at_y, GX + GZ)

    lane = iota((1, 128), 1)
    m = [jnp.sum(jnp.where(lane == k, row, 0.0), axis=1, keepdims=True) for k in range(6)]

    def form(coefficients, shift):
        total = None
        for i, left in enumerate(coefficients):
            for j, right in enumerate(coefficients):
                term = left * right * m[i + j + shift]
                total = term if total is None else total + term
        return total

    one = jnp.ones_like(m[0])
    rr = m[0]
    direction = [one]
    residual = [one]
    solution_row = [jnp.zeros_like(one)] * 3
    for step in range(3):
        alpha = rr / form(direction, 1)
        for i, value in enumerate(direction):
            solution_row[i] = solution_row[i] + alpha * value
        if step == 2:
            break
        residual = residual + [jnp.zeros_like(one)]
        for i, value in enumerate(direction):
            residual[i + 1] = residual[i + 1] - alpha * value
        new = form(residual, 0)
        beta = new / rr
        direction = [
            value + beta * direction[i] if i < len(direction) else value
            for i, value in enumerate(residual)
        ]
        rr = new
    p_out[...] = (solution_row[0] * v0 + solution_row[1] * v1 + solution_row[2] * v2) * SCALE

    for copy in to_home:
        copy.wait_recv()
    back = jnp.concatenate([recvv[g] for g in range(GY)], axis=0)
    spread = jnp.dot(back, slots, precision=EXACT, preferred_element_type=F32)
    velocity = jnp.zeros((8, 512), F32)
    for g in range(GY):
        velocity = velocity + spread[8 * g : 8 * g + 8, :] * owned[g : g + 1, :]
    pv_out[...] = velocity[0:3, :]

    for copy in sends:
        copy.wait_send()


def body(vel, src, met, scr, coords, owner, elem):
    table = np.array(deriv_table(), np.float32)
    kron = np.kron(np.eye(16, dtype=np.float32), table)
    lsc = np.repeat(np.array(lagrange_scale(), np.float32)[:, None], 128, axis=1)
    operands = (
        vel.reshape(3, 128, 128),
        src.reshape(128, 128),
        met.reshape(3, 128, 128),
        scr.reshape(128, 128),
        coords,
        owner.reshape(1, 512),
        elem.reshape(1, 512),
        jnp.asarray(kron),
        jnp.asarray(kron.T),
        jnp.asarray(kron),
        jnp.asarray(kron.T),
        jnp.asarray(lsc),
    )
    vmem = pl.BlockSpec(memory_space=pltpu.VMEM)
    dma = pltpu.SemaphoreType.DMA
    pressure, velocity = pl.pallas_call(
        kernel,
        out_shape=(
            jax.ShapeDtypeStruct((128, 128), F32),
            jax.ShapeDtypeStruct((3, 512), F32),
        ),
        in_specs=[vmem] * len(operands),
        out_specs=(vmem, vmem),
        scratch_shapes=[
            pltpu.VMEM((FIELDS, 128, 128), F32),
            pltpu.VMEM((2, 2, 16, 128), F32),
            pltpu.VMEM((FIELDS, 2, 16, 128), F32),
            pltpu.VMEM((FIELDS, 2, 8, 128), F32),
            pltpu.VMEM((FIELDS, 2, 8, 128), F32),
            pltpu.VMEM((FIELDS, 2, 1, 128), F32),
            pltpu.VMEM((FIELDS, 2, 1, 128), F32),
            dma((FIELDS, 6)),
            dma((FIELDS, 6)),
            pltpu.VMEM((3, 1, 128), F32),
            pltpu.VMEM((GX, 1, 128), F32),
            pltpu.VMEM((GZ, 1, 128), F32),
            pltpu.VMEM((GY, 1, 128), F32),
            dma((GX + GY + GZ,)),
            dma((GX + GY + GZ,)),
            pltpu.VMEM((GY, 8, 128), F32),
            pltpu.VMEM((GY, 8, 128), F32),
            pltpu.VMEM((GY, 8, 128), F32),
            pltpu.VMEM((GY, 8, 128), F32),
            dma((2, GY)),
            dma((2, GY)),
            pltpu.VMEM((384, 128), BF16),
            pltpu.VMEM((384, 128), BF16),
        ],
        compiler_params=pltpu.CompilerParams(collective_id=0, has_side_effects=True),
        name="step",
    )(*operands)
    return pressure.reshape(8, 16, 128), velocity


def solution(mesh):
    in_specs = (
        P(None, "gx", "gy", "gz"),
        P("gx", "gy", "gz"),
        P(None, "gx", "gy", "gz"),
        P("gx", "gy", "gz"),
        P(None, ("gx", "gy", "gz")),
        P(("gx", "gy", "gz"), None),
        P(("gx", "gy", "gz")),
    )
    out_specs = (P("gx", "gy", "gz"), P(None, ("gx", "gy", "gz")))
    return jax.shard_map(body, mesh=mesh, in_specs=in_specs, out_specs=out_specs, check_vma=False)
```

```python
import itertools

import jax
import jax.numpy as jnp
import numpy as np
from jax import lax
from jax.experimental import pallas as pl
from jax.experimental.pallas import tpu as pltpu
from jax.sharding import PartitionSpec as P

MESH = pl.DeviceIdType.MESH
F32 = jnp.float32
BF16 = jnp.bfloat16
EXACT = lax.Precision.HIGHEST
SCALE = 1.0 / 64.0
GX, GY, GZ = 4, 16, 8
CAP = 128


def gll_points():
    return [
        -1.0,
        -0.8717401485096066,
        -0.5917001814331423,
        -0.2092992179024789,
        0.2092992179024789,
        0.5917001814331423,
        0.8717401485096066,
        1.0,
    ]


def legendre_seven(point):
    before, current = (1.0, point)
    for order in range(1, 7):
        before, current = (
            current,
            ((2 * order + 1) * point * current - order * before) / (order + 1),
        )
    return current


def deriv_table():
    points = gll_points()
    legendre = [legendre_seven(value) for value in points]
    derivative = [[0.0] * 8 for row in range(8)]
    for i in range(8):
        for j in range(8):
            if i != j:
                derivative[i][j] = legendre[i] / legendre[j] / (points[i] - points[j])
    derivative[0][0] = -14.0
    derivative[7][7] = 14.0
    return derivative


def lagrange_scale():
    points = gll_points()
    scale = []
    for i in range(8):
        product = 1.0
        for m in range(8):
            if m != i:
                product *= points[i] - points[m]
        scale.append(1.0 / product)
    return scale


def iota(shape, dim):
    return lax.broadcasted_iota(jnp.int32, shape, dim)


DIRECTIONS = sorted(
    (d for d in itertools.product((-1, 0, 1), repeat=3) if any(d)),
    key=lambda d: -sum(abs(v) for v in d),
)
RING_Y = [k for k in range(2, GY - 1)]


def kernel(
    vel_in, src_in, met_in, scr_in, coords_in, owner_in, elem_in, ky_in, kyt_in, lsc_in,
    p_out, pv_out,
    vel, src, met, scr, coords, owner, elem, ky, kyt, lsc, load_sem,
    work, hxs, hx, hys, hyr, hes, her, hzs, hzr, hss, hrs,
    vhx, vys, vyr, vzs, vzr, vss, vrs,
    msg, rxz, ry, ass, ars,
    sendp, recvp, sendv, recvv, pss, prs, vhi, vlo,
):
    gx, gy, gz = lax.axis_index("gx"), lax.axis_index("gy"), lax.axis_index("gz")

    def at_x(k):
        return (lax.rem(gx + (k + GX), GX), gy, gz)

    def at_y(k):
        return (gx, lax.rem(gy + (k + GY), GY), gz)

    def at_z(k):
        return (gx, gy, lax.rem(gz + (k + GZ), GZ))

    def near(d):
        return (
            lax.rem(gx + (d[0] + GX), GX),
            lax.rem(gy + (d[1] + GY), GY),
            lax.rem(gz + (d[2] + GZ), GZ),
        )

    barrier = pltpu.get_barrier_semaphore()
    for d in DIRECTIONS:
        pl.semaphore_signal(barrier, inc=1, device_id=near(d), device_id_type=MESH)
    for k in RING_Y:
        pl.semaphore_signal(barrier, inc=1, device_id=at_y(k), device_id_type=MESH)

    loads = {}
    for i, (name, source, target) in enumerate((
        ("src", src_in, src), ("vel", vel_in, vel), ("ky", ky_in, ky), ("kyt", kyt_in, kyt),
        ("met", met_in, met), ("scr", scr_in, scr), ("coords", coords_in, coords),
        ("owner", owner_in, owner), ("elem", elem_in, elem), ("lsc", lsc_in, lsc),
    )):
        loads[name] = pltpu.make_async_copy(source, target, load_sem.at[i])
        loads[name].start()

    sends = []

    def remote(src_ref, dst_ref, ssem, rsem, device):
        copy = pltpu.make_async_remote_copy(
            src_ref=src_ref,
            dst_ref=dst_ref,
            send_sem=ssem,
            recv_sem=rsem,
            device_id=device,
            device_id_type=MESH,
        )
        copy.start()
        sends.append(copy)
        return copy

    row_id = iota((128, 128), 0)
    lane_id = iota((128, 128), 1)
    eye = row_id == lane_id
    lane_in = lane_id % 8
    low_z = (lane_in == 0) & (lane_id > 0)
    high_z = (lane_in == 7) & (lane_id < 127)
    at_floor = gy == 0
    at_ceiling = gy == GY - 1

    def source_mask():
        index = iota((16, 128), 0)
        lane = iota((16, 128), 1)
        from_x, from_y = index // 3 - 1, index % 3 - 1
        in_x, in_y = lane // 16, lane % 16
        keep = (index < 9) & jnp.logical_not((from_y == -1) & at_floor)
        keep = keep & jnp.logical_not((from_y == 1) & at_ceiling)
        keep = keep & ((from_x == 0) | ((from_x == -1) & (in_x == 0)) | ((from_x == 1) & (in_x == 7)))
        return keep & ((from_y == 0) | ((from_y == -1) & (in_y == 0)) | ((from_y == 1) & (in_y == 15)))

    z_keep = source_mask()

    def start_halo(f, field):
        w = work.at[f]
        w[...] = field
        both = w[pl.ds(7, 8, stride=16), :] + w[pl.ds(8, 8, stride=16), :]
        w[pl.ds(7, 8, stride=16), :] = both
        w[pl.ds(8, 8, stride=16), :] = both
        field = w[...]
        pair = jnp.concatenate(
            [
                jnp.sum(jnp.where(eye, field[:, 127:128], 0.0), axis=0, keepdims=True),
                jnp.sum(jnp.where(eye, field[:, 0:1], 0.0), axis=0, keepdims=True),
            ],
            axis=0,
        )
        for dx in (-1, 0, 1):
            for dy in (-1, 0, 1):
                shift = (16 * dx - 15 * dy) % 128
                hzs[f, (1 - dx) * 3 + (1 - dy)] = pltpu.roll(pair, shift, 1) if shift else pair
        copies = {}

        def send(d, source, target):
            k = DIRECTIONS.index(d)
            copies[d] = remote(source, target, hss.at[f, k], hrs.at[f, k], near(d))

        for d in DIRECTIONS:
            if d[2]:
                j, side = (1 - d[0]) * 3 + (1 - d[1]), (1 - d[2]) // 2
                send(d, hzs.at[f, j, pl.ds(side, 1)], hzr.at[f, side, pl.ds(j, 1)])
        field = (
            field
            + jnp.where(low_z, pltpu.roll(field, 1, 1), 0.0)
            + jnp.where(high_z, pltpu.roll(field, 127, 1), 0.0)
        )
        w[...] = field
        for d in DIRECTIONS:
            if d[2] == 0 and d[0] and d[1]:
                e = (1 - d[0]) + (1 - d[1]) // 2
                row = (112 if d[0] == 1 else 0) + (15 if d[1] == 1 else 0)
                hes[f, e] = field[row : row + 1, :]
                send(d, hes.at[f, e], her.at[f, e])
        hxs[f, 0] = field[112:128, :]
        hxs[f, 1] = field[0:16, :]
        send((1, 0, 0), hxs.at[f, 0], hx.at[f, 0])
        send((-1, 0, 0), hxs.at[f, 1], hx.at[f, 1])
        hys[f, 0] = w[pl.ds(15, 8, stride=16), :]
        hys[f, 1] = w[pl.ds(0, 8, stride=16), :]
        send((0, 1, 0), hys.at[f, 0], hyr.at[f, 0])
        send((0, -1, 0), hys.at[f, 1], hyr.at[f, 1])
        return copies

    def end_halo(f, copies):
        w = work.at[f]
        copies[0, 1, 0].wait_recv()
        w[pl.ds(0, 8, stride=16), :] = w[pl.ds(0, 8, stride=16), :] + jnp.where(at_floor, 0.0, hyr[f, 0])
        copies[0, -1, 0].wait_recv()
        w[pl.ds(15, 8, stride=16), :] = w[pl.ds(15, 8, stride=16), :] + jnp.where(at_ceiling, 0.0, hyr[f, 1])
        copies[1, 0, 0].wait_recv()
        w[pl.ds(0, 16), :] = w[pl.ds(0, 16), :] + hx[f, 0]
        copies[-1, 0, 0].wait_recv()
        w[pl.ds(112, 16), :] = w[pl.ds(112, 16), :] + hx[f, 1]
        for d in DIRECTIONS:
            if d[2] == 0 and d[0] and d[1]:
                e = (1 - d[0]) + (1 - d[1]) // 2
                row = (0 if d[0] == 1 else 112) + (0 if d[1] == 1 else 15)
                copies[d].wait_recv()
                cut = at_floor if d[1] == 1 else at_ceiling
                w[pl.ds(row, 1), :] = w[pl.ds(row, 1), :] + jnp.where(cut, 0.0, her[f, e])
        field = w[...]
        for d in reversed(DIRECTIONS):
            if d[2]:
                copies[d].wait_recv()
        low = jnp.sum(jnp.where(z_keep, hzr[f, 0], 0.0), axis=0, keepdims=True)
        high = jnp.sum(jnp.where(z_keep, hzr[f, 1], 0.0), axis=0, keepdims=True)
        low = jnp.sum(jnp.where(eye, low, 0.0), axis=1, keepdims=True)
        high = jnp.sum(jnp.where(eye, high, 0.0), axis=1, keepdims=True)
        return field + jnp.where(lane_id == 0, low, 0.0) + jnp.where(lane_id == 127, high, 0.0)

    def start_x(c):
        return (
            remote(vel.at[c, pl.ds(112, 16)], vhx.at[c, 0], vss.at[c, 0], vrs.at[c, 0], at_x(1)),
            remote(vel.at[c, pl.ds(0, 16)], vhx.at[c, 1], vss.at[c, 1], vrs.at[c, 1], at_x(-1)),
        )

    def mid_xy(c, copies):
        w = work.at[3 + c]
        w[...] = vel[c]
        copies[0].wait_recv()
        w[pl.ds(0, 16), :] = w[pl.ds(0, 16), :] + vhx[c, 0]
        copies[1].wait_recv()
        w[pl.ds(112, 16), :] = w[pl.ds(112, 16), :] + vhx[c, 1]
        both = w[pl.ds(7, 8, stride=16), :] + w[pl.ds(8, 8, stride=16), :]
        w[pl.ds(7, 8, stride=16), :] = both
        w[pl.ds(8, 8, stride=16), :] = both
        vys[c, 0] = w[pl.ds(15, 8, stride=16), :]
        vys[c, 1] = w[pl.ds(0, 8, stride=16), :]
        return (
            remote(vys.at[c, 0], vyr.at[c, 0], vss.at[c, 2], vrs.at[c, 2], at_y(1)),
            remote(vys.at[c, 1], vyr.at[c, 1], vss.at[c, 3], vrs.at[c, 3], at_y(-1)),
        )

    def mid_yz(c, copies):
        w = work.at[3 + c]
        copies[0].wait_recv()
        w[pl.ds(0, 8, stride=16), :] = w[pl.ds(0, 8, stride=16), :] + jnp.where(at_floor, 0.0, vyr[c, 0])
        copies[1].wait_recv()
        w[pl.ds(15, 8, stride=16), :] = w[pl.ds(15, 8, stride=16), :] + jnp.where(at_ceiling, 0.0, vyr[c, 1])
        field = w[...]
        vzs[c, 0] = jnp.sum(jnp.where(eye, field[:, 127:128], 0.0), axis=0, keepdims=True)
        vzs[c, 1] = jnp.sum(jnp.where(eye, field[:, 0:1], 0.0), axis=0, keepdims=True)
        out = (
            remote(vzs.at[c, 0], vzr.at[c, 0], vss.at[c, 4], vrs.at[c, 4], at_z(1)),
            remote(vzs.at[c, 1], vzr.at[c, 1], vss.at[c, 5], vrs.at[c, 5], at_z(-1)),
        )
        w[...] = (
            field
            + jnp.where(low_z, pltpu.roll(field, 1, 1), 0.0)
            + jnp.where(high_z, pltpu.roll(field, 127, 1), 0.0)
        )
        return out

    def end_z(c, copies):
        field = work[3 + c]
        copies[0].wait_recv()
        low = jnp.sum(jnp.where(eye, vzr[c, 0], 0.0), axis=1, keepdims=True)
        copies[1].wait_recv()
        high = jnp.sum(jnp.where(eye, vzr[c, 1], 0.0), axis=1, keepdims=True)
        field = field + jnp.where(lane_id == 0, low, 0.0) + jnp.where(lane_id == 127, high, 0.0)
        high = field.astype(BF16)
        vhi[pl.ds(128 * c, 128), :] = high
        vlo[pl.ds(128 * c, 128), :] = (field - high.astype(F32)).astype(BF16)

    table = deriv_table()

    def along_x(field, transposed):
        parts = [field[16 * i : 16 * i + 16, :] for i in range(8)]
        out = []
        for a in range(8):
            total = None
            for i in range(8):
                factor = table[i][a] if transposed else table[a][i]
                if factor == 0.0:
                    continue
                term = parts[i] * np.float32(factor)
                total = term if total is None else total + term
            out.append(total)
        return jnp.concatenate(out, axis=0)

    def gradients(field):
        return (
            along_x(field, False),
            jnp.dot(ky[...], field, precision=EXACT, preferred_element_type=F32),
            jnp.dot(field, kyt[...], precision=EXACT, preferred_element_type=F32),
        )

    def operator(field):
        dx, dy, dz = gradients(field)
        return (
            along_x(met[0] * dx, True)
            + jnp.dot(kyt[...], met[1] * dy, precision=EXACT, preferred_element_type=F32)
            + jnp.dot(met[2] * dz, ky[...], precision=EXACT, preferred_element_type=F32)
            + scr[...] * field
        ) * SCALE

    sendv[...] = jnp.zeros_like(sendv)
    loads["src"].wait()
    pl.semaphore_wait(barrier, len(DIRECTIONS) + len(RING_Y))
    halo = start_halo(0, src[...])
    loads["vel"].wait()
    cvx = [start_x(c) for c in range(3)]

    loads["coords"].wait()
    loads["owner"].wait()
    loads["elem"].wait()
    owned = (owner[...] == iota((GY, 512), 0)).astype(F32)
    tri = (iota((128, 128), 0) < iota((128, 128), 1)).astype(BF16)
    before = jnp.zeros((GY, 1), F32)
    rank = []
    for b in range(4):
        part = owned[:, 128 * b : 128 * b + 128]
        count = jnp.dot(part.astype(BF16), tri, preferred_element_type=F32) + before
        rank.append(jnp.sum(count * part, axis=0, keepdims=True))
        before = before + jnp.sum(part, axis=1, keepdims=True)
    rank = jnp.concatenate(rank, axis=1)
    slots = (rank.astype(jnp.int32) == iota((CAP, 512), 0)).astype(F32)
    data = jnp.concatenate(
        [coords[...], elem[...].astype(F32), jnp.zeros((4, 512), F32)], axis=0
    )
    lhs = jnp.concatenate([data * owned[g : g + 1, :] for g in range(GY)], axis=0)
    packed = lax.dot_general(
        lhs, slots, (((1,), (1,)), ((), ())), precision=EXACT, preferred_element_type=F32
    )
    for g in range(GY):
        sendp[g] = packed[8 * g : 8 * g + 8, :]

    to_owner = []
    for k in range(1, GY):
        peer = lax.rem(gy + k, GY)
        to_owner.append(
            remote(sendp.at[peer], recvp.at[gy], pss.at[0, k], prs.at[0, k], (gx, peer, gz))
        )
    recvp[gy] = sendp[gy]

    cvy = [mid_xy(c, cvx[c]) for c in range(3)]
    loads["ky"].wait()
    loads["kyt"].wait()
    loads["met"].wait()
    loads["scr"].wait()
    v0 = end_halo(0, halo)

    halo = start_halo(1, operator(v0))
    cvz = [mid_yz(c, cvy[c]) for c in range(3)]
    v1 = end_halo(1, halo)
    halo = start_halo(2, operator(v1))
    for c in range(3):
        end_z(c, cvz[c])

    loads["lsc"].wait()
    for copy in to_owner:
        copy.wait_recv()
    points = gll_points()
    node = iota((8, 128), 0)

    def basis(coord):
        product = lsc[...]
        for m in range(8):
            product = product * jnp.where(node == m, 1.0, coord - np.float32(points[m]))
        return product

    def sample_two(step, carry):
        low_parts, high_parts, weights = [], [], []
        for half in range(2):
            block = recvp[2 * step + half]
            element = block[3:4, :].astype(jnp.int32)
            bx, by, bz = (basis(block[d : d + 1, :]) for d in range(3))
            element_y = element // 16
            element_z = element % 16
            wide = jnp.concatenate(
                [jnp.where(element_z == e, bz, 0.0) for e in range(16)], axis=0
            )
            high = wide.astype(BF16)
            high_parts.append(high)
            low_parts.append((wide - high.astype(F32)).astype(BF16))
            tall = jnp.concatenate(
                [jnp.where(element_y == e, by, 0.0) for e in range(2)], axis=0
            )
            weights.append(
                jnp.concatenate([bx[i : i + 1, :] * tall for i in range(8)], axis=0)
            )
        high = jnp.concatenate(high_parts, axis=1)
        low = jnp.concatenate(low_parts, axis=1)
        for c in range(3):
            vh = vhi[pl.ds(128 * c, 128), :]
            partial = (
                jnp.dot(vh, high, preferred_element_type=F32)
                + jnp.dot(vh, low, preferred_element_type=F32)
                + jnp.dot(vlo[pl.ds(128 * c, 128), :], high, preferred_element_type=F32)
            )
            for half in range(2):
                sendv[2 * step + half, pl.ds(c, 1), :] = jnp.sum(
                    partial[:, 128 * half : 128 * half + 128] * weights[half], axis=0, keepdims=True
                )
        return carry

    lax.fori_loop(0, GY // 2, sample_two, 0)

    to_home = []
    for k in range(1, GY):
        peer = lax.rem(gy + k, GY)
        to_home.append(
            remote(sendv.at[peer], recvv.at[gy], pss.at[1, k], prs.at[1, k], (gx, peer, gz))
        )
    recvv[gy] = sendv[gy]
    v2 = end_halo(2, halo)

    place_y = row_id % 16
    share_x = jnp.where((row_id < 16) | (row_id >= 112), 0.5, 1.0)
    edge_y = (place_y % 8 == 0) | (place_y % 8 == 7)
    wall = ((place_y == 0) & at_floor) | ((place_y == 15) & at_ceiling)
    share_y = jnp.where(edge_y & jnp.logical_not(wall), 0.5, 1.0)
    share_z = jnp.where((lane_in == 0) | (lane_in == 7), 0.5, 1.0)
    weight = share_x * share_y * share_z
    dx, dy, dz = gradients(v2)
    products = [
        weight * v0 * v0,
        weight * v0 * v1,
        weight * v1 * v1,
        weight * v1 * v2,
        weight * v2 * v2,
        (met[0] * dx * dx + met[1] * dy * dy + met[2] * dz * dz + scr[...] * v2 * v2) * SCALE,
    ]
    rows = [jnp.sum(value, axis=0, keepdims=True) for value in products]
    rows = jnp.concatenate(rows + [jnp.zeros((2, 128), F32)], axis=0)
    total = jnp.sum(rows, axis=1, keepdims=True)
    row = jnp.sum(
        jnp.where(iota((8, 128), 0) == iota((8, 128), 1), total, 0.0), axis=0, keepdims=True
    )

    msg[0] = row
    here = gx * GZ + gz
    rxz[here] = row
    copies = []
    for i in range(GX):
        for k in range(GZ):
            if i or k:
                n = i * GZ + k
                device = (lax.rem(gx + i, GX), gy, lax.rem(gz + k, GZ))
                copies.append(remote(msg.at[0], rxz.at[here], ass.at[n], ars.at[n], device))
    for copy in copies:
        copy.wait_recv()
    row = jnp.sum(rxz[...], axis=0)
    msg[1] = row
    ry[gy] = row
    copies = []
    for k in range(1, GY):
        n = GX * GZ + k
        copies.append(remote(msg.at[1], ry.at[gy], ass.at[n], ars.at[n], at_y(k)))

    for copy in to_home:
        copy.wait_recv()
    back = jnp.concatenate([recvv[g] for g in range(GY)], axis=0)
    spread = jnp.dot(back, slots, precision=EXACT, preferred_element_type=F32)
    velocity = jnp.zeros((8, 512), F32)
    for g in range(GY):
        velocity = velocity + spread[8 * g : 8 * g + 8, :] * owned[g : g + 1, :]
    pv_out[...] = velocity[0:3, :]

    for copy in copies:
        copy.wait_recv()
    row = jnp.sum(ry[...], axis=0)

    lane = iota((1, 128), 1)
    m = [jnp.sum(jnp.where(lane == k, row, 0.0), axis=1, keepdims=True) for k in range(6)]

    def form(coefficients, shift):
        total = None
        for i, left in enumerate(coefficients):
            for j, right in enumerate(coefficients):
                term = left * right * m[i + j + shift]
                total = term if total is None else total + term
        return total

    one = jnp.ones_like(m[0])
    rr = m[0]
    direction = [one]
    residual = [one]
    solution_row = [jnp.zeros_like(one)] * 3
    for step in range(3):
        alpha = rr / form(direction, 1)
        for i, value in enumerate(direction):
            solution_row[i] = solution_row[i] + alpha * value
        if step == 2:
            break
        residual = residual + [jnp.zeros_like(one)]
        for i, value in enumerate(direction):
            residual[i + 1] = residual[i + 1] - alpha * value
        new = form(residual, 0)
        beta = new / rr
        direction = [
            value + beta * direction[i] if i < len(direction) else value
            for i, value in enumerate(residual)
        ]
        rr = new
    p_out[...] = (solution_row[0] * v0 + solution_row[1] * v1 + solution_row[2] * v2) * SCALE

    for copy in sends:
        copy.wait_send()


def body(vel, src, met, scr, coords, owner, elem):
    table = np.array(deriv_table(), np.float32)
    kron = np.kron(np.eye(16, dtype=np.float32), table)
    lsc = np.repeat(np.array(lagrange_scale(), np.float32)[:, None], 128, axis=1)
    operands = (
        vel.reshape(3, 128, 128),
        src.reshape(128, 128),
        met.reshape(3, 128, 128),
        scr.reshape(128, 128),
        coords,
        owner.reshape(1, 512),
        elem.reshape(1, 512),
        jnp.asarray(kron),
        jnp.asarray(kron.T),
        jnp.asarray(lsc),
    )
    anywhere = pl.BlockSpec(memory_space=pl.ANY)
    vmem = pl.BlockSpec(memory_space=pltpu.VMEM)
    dma = pltpu.SemaphoreType.DMA
    pressure, velocity = pl.pallas_call(
        kernel,
        out_shape=(
            jax.ShapeDtypeStruct((128, 128), F32),
            jax.ShapeDtypeStruct((3, 512), F32),
        ),
        in_specs=[anywhere] * len(operands),
        out_specs=(vmem, vmem),
        scratch_shapes=[pltpu.VMEM(x.shape, x.dtype) for x in operands]
        + [
            dma((len(operands),)),
            pltpu.VMEM((6, 128, 128), F32),
            pltpu.VMEM((3, 2, 16, 128), F32),
            pltpu.VMEM((3, 2, 16, 128), F32),
            pltpu.VMEM((3, 2, 8, 128), F32),
            pltpu.VMEM((3, 2, 8, 128), F32),
            pltpu.VMEM((3, 4, 1, 128), F32),
            pltpu.VMEM((3, 4, 1, 128), F32),
            pltpu.VMEM((3, 9, 2, 128), F32),
            pltpu.VMEM((3, 2, 16, 128), F32),
            dma((3, 26)),
            dma((3, 26)),
            pltpu.VMEM((3, 2, 16, 128), F32),
            pltpu.VMEM((3, 2, 8, 128), F32),
            pltpu.VMEM((3, 2, 8, 128), F32),
            pltpu.VMEM((3, 2, 1, 128), F32),
            pltpu.VMEM((3, 2, 1, 128), F32),
            dma((3, 6)),
            dma((3, 6)),
            pltpu.VMEM((2, 1, 128), F32),
            pltpu.VMEM((GX * GZ, 1, 128), F32),
            pltpu.VMEM((GY, 1, 128), F32),
            dma((GX * GZ + GY,)),
            dma((GX * GZ + GY,)),
            pltpu.VMEM((GY, 8, 128), F32),
            pltpu.VMEM((GY, 8, 128), F32),
            pltpu.VMEM((GY, 8, 128), F32),
            pltpu.VMEM((GY, 8, 128), F32),
            dma((2, GY)),
            dma((2, GY)),
            pltpu.VMEM((384, 128), BF16),
            pltpu.VMEM((384, 128), BF16),
        ],
        compiler_params=pltpu.CompilerParams(collective_id=0, has_side_effects=True),
        name="step",
    )(*operands)
    return pressure.reshape(8, 16, 128), velocity


def solution(mesh):
    in_specs = (
        P(None, "gx", "gy", "gz"),
        P("gx", "gy", "gz"),
        P(None, "gx", "gy", "gz"),
        P("gx", "gy", "gz"),
        P(None, ("gx", "gy", "gz")),
        P(("gx", "gy", "gz"), None),
        P(("gx", "gy", "gz")),
    )
    out_specs = (P("gx", "gy", "gz"), P(None, ("gx", "gy", "gz")))
    return jax.shard_map(body, mesh=mesh, in_specs=in_specs, out_specs=out_specs, check_vma=False)
```

```python
import itertools

import jax
import jax.numpy as jnp
import numpy as np
from jax import lax
from jax.experimental import pallas as pl
from jax.experimental.pallas import tpu as pltpu
from jax.sharding import PartitionSpec as P

MESH = pl.DeviceIdType.MESH
F32 = jnp.float32
BF16 = jnp.bfloat16
EXACT = lax.Precision.HIGHEST
SCALE = 1.0 / 64.0
GX, GY, GZ = 4, 16, 8
CAP = 128


def gll_points():
    return [
        -1.0,
        -0.8717401485096066,
        -0.5917001814331423,
        -0.2092992179024789,
        0.2092992179024789,
        0.5917001814331423,
        0.8717401485096066,
        1.0,
    ]


def legendre_seven(point):
    before, current = (1.0, point)
    for order in range(1, 7):
        before, current = (
            current,
            ((2 * order + 1) * point * current - order * before) / (order + 1),
        )
    return current


def deriv_table():
    points = gll_points()
    legendre = [legendre_seven(value) for value in points]
    derivative = [[0.0] * 8 for row in range(8)]
    for i in range(8):
        for j in range(8):
            if i != j:
                derivative[i][j] = legendre[i] / legendre[j] / (points[i] - points[j])
    derivative[0][0] = -14.0
    derivative[7][7] = 14.0
    return derivative


def lagrange_scale():
    points = gll_points()
    scale = []
    for i in range(8):
        product = 1.0
        for m in range(8):
            if m != i:
                product *= points[i] - points[m]
        scale.append(1.0 / product)
    return scale


def iota(shape, dim):
    return lax.broadcasted_iota(jnp.int32, shape, dim)


DIRECTIONS = sorted(
    (d for d in itertools.product((-1, 0, 1), repeat=3) if any(d)),
    key=lambda d: -sum(abs(v) for v in d),
)
RING_Y = [k for k in range(2, GY - 1)]


def kernel(
    vel_in, src_in, met_in, scr_in, coords_in, owner_in, elem_in, ky_in, kyt_in, lsc_in,
    p_out, pv_out,
    vel, src, met, scr, coords, owner, elem, ky, kyt, lsc, load_sem,
    work, hxs, hx, hys, hyr, hes, her, hzs, hzr, hss, hrs,
    vhx, vys, vyr, vzs, vzr, vss, vrs,
    msg, rxz, ry, ass, ars,
    sendp, recvp, sendv, recvv, pss, prs, vhi, vlo,
):
    gx, gy, gz = lax.axis_index("gx"), lax.axis_index("gy"), lax.axis_index("gz")

    def at_x(k):
        return (lax.rem(gx + (k + GX), GX), gy, gz)

    def at_y(k):
        return (gx, lax.rem(gy + (k + GY), GY), gz)

    def at_z(k):
        return (gx, gy, lax.rem(gz + (k + GZ), GZ))

    def near(d):
        return (
            lax.rem(gx + (d[0] + GX), GX),
            lax.rem(gy + (d[1] + GY), GY),
            lax.rem(gz + (d[2] + GZ), GZ),
        )

    barrier = pltpu.get_barrier_semaphore()
    for d in DIRECTIONS:
        pl.semaphore_signal(barrier, inc=1, device_id=near(d), device_id_type=MESH)
    for k in RING_Y:
        pl.semaphore_signal(barrier, inc=1, device_id=at_y(k), device_id_type=MESH)

    loads = {}
    for i, (name, source, target) in enumerate((
        ("src", src_in, src), ("vel", vel_in, vel), ("ky", ky_in, ky), ("kyt", kyt_in, kyt),
        ("met", met_in, met), ("scr", scr_in, scr), ("coords", coords_in, coords),
        ("owner", owner_in, owner), ("elem", elem_in, elem), ("lsc", lsc_in, lsc),
    )):
        loads[name] = pltpu.make_async_copy(source, target, load_sem.at[i])
        loads[name].start()

    sends = []

    def remote(src_ref, dst_ref, ssem, rsem, device):
        copy = pltpu.make_async_remote_copy(
            src_ref=src_ref,
            dst_ref=dst_ref,
            send_sem=ssem,
            recv_sem=rsem,
            device_id=device,
            device_id_type=MESH,
        )
        copy.start()
        sends.append(copy)
        return copy

    row_id = iota((128, 128), 0)
    lane_id = iota((128, 128), 1)
    eye = row_id == lane_id
    lane_in = lane_id % 8
    low_z = (lane_in == 0) & (lane_id > 0)
    high_z = (lane_in == 7) & (lane_id < 127)
    at_floor = gy == 0
    at_ceiling = gy == GY - 1

    def source_mask():
        index = iota((16, 128), 0)
        lane = iota((16, 128), 1)
        from_x, from_y = index // 3 - 1, index % 3 - 1
        in_x, in_y = lane // 16, lane % 16
        keep = (index < 9) & jnp.logical_not((from_y == -1) & at_floor)
        keep = keep & jnp.logical_not((from_y == 1) & at_ceiling)
        keep = keep & ((from_x == 0) | ((from_x == -1) & (in_x == 0)) | ((from_x == 1) & (in_x == 7)))
        return keep & ((from_y == 0) | ((from_y == -1) & (in_y == 0)) | ((from_y == 1) & (in_y == 15)))

    z_keep = source_mask()

    def pack_planes(f, field):
        w = work.at[f]
        w[...] = field
        both = w[pl.ds(7, 8, stride=16), :] + w[pl.ds(8, 8, stride=16), :]
        w[pl.ds(7, 8, stride=16), :] = both
        w[pl.ds(8, 8, stride=16), :] = both
        field = w[...]
        pair = jnp.concatenate(
            [
                jnp.sum(jnp.where(eye, field[:, 127:128], 0.0), axis=0, keepdims=True),
                jnp.sum(jnp.where(eye, field[:, 0:1], 0.0), axis=0, keepdims=True),
            ],
            axis=0,
        )
        for dx in (-1, 0, 1):
            for dy in (-1, 0, 1):
                shift = (16 * dx - 15 * dy) % 128
                hzs[f, (1 - dx) * 3 + (1 - dy)] = pltpu.roll(pair, shift, 1) if shift else pair
        return field

    def pack_faces(f, field):
        w = work.at[f]
        field = (
            field
            + jnp.where(low_z, pltpu.roll(field, 1, 1), 0.0)
            + jnp.where(high_z, pltpu.roll(field, 127, 1), 0.0)
        )
        w[...] = field
        for d in DIRECTIONS:
            if d[2] == 0 and d[0] and d[1]:
                row = (112 if d[0] == 1 else 0) + (15 if d[1] == 1 else 0)
                hes[f, (1 - d[0]) + (1 - d[1]) // 2] = field[row : row + 1, :]
        hxs[f, 0] = field[112:128, :]
        hxs[f, 1] = field[0:16, :]
        hys[f, 0] = w[pl.ds(15, 8, stride=16), :]
        hys[f, 1] = w[pl.ds(0, 8, stride=16), :]

    def send_halo(f, copies, planes):
        for d in DIRECTIONS:
            if planes != (d[2] != 0):
                continue
            k = DIRECTIONS.index(d)
            if d[2]:
                j, side = (1 - d[0]) * 3 + (1 - d[1]), (1 - d[2]) // 2
                source, target = hzs.at[f, j, pl.ds(side, 1)], hzr.at[f, side, pl.ds(j, 1)]
            elif d[0] and d[1]:
                e = (1 - d[0]) + (1 - d[1]) // 2
                source, target = hes.at[f, e], her.at[f, e]
            elif d[0]:
                source, target = hxs.at[f, (1 - d[0]) // 2], hx.at[f, (1 - d[0]) // 2]
            else:
                source, target = hys.at[f, (1 - d[1]) // 2], hyr.at[f, (1 - d[1]) // 2]
            copies[d] = remote(source, target, hss.at[f, k], hrs.at[f, k], near(d))

    def start_halo(f, field):
        copies = {}
        field = pack_planes(f, field)
        send_halo(f, copies, True)
        pack_faces(f, field)
        send_halo(f, copies, False)
        return copies

    def end_halo(f, copies):
        w = work.at[f]
        copies[0, 1, 0].wait_recv()
        w[pl.ds(0, 8, stride=16), :] = w[pl.ds(0, 8, stride=16), :] + jnp.where(at_floor, 0.0, hyr[f, 0])
        copies[0, -1, 0].wait_recv()
        w[pl.ds(15, 8, stride=16), :] = w[pl.ds(15, 8, stride=16), :] + jnp.where(at_ceiling, 0.0, hyr[f, 1])
        copies[1, 0, 0].wait_recv()
        w[pl.ds(0, 16), :] = w[pl.ds(0, 16), :] + hx[f, 0]
        copies[-1, 0, 0].wait_recv()
        w[pl.ds(112, 16), :] = w[pl.ds(112, 16), :] + hx[f, 1]
        for d in DIRECTIONS:
            if d[2] == 0 and d[0] and d[1]:
                e = (1 - d[0]) + (1 - d[1]) // 2
                row = (0 if d[0] == 1 else 112) + (0 if d[1] == 1 else 15)
                copies[d].wait_recv()
                cut = at_floor if d[1] == 1 else at_ceiling
                w[pl.ds(row, 1), :] = w[pl.ds(row, 1), :] + jnp.where(cut, 0.0, her[f, e])
        field = w[...]
        for d in reversed(DIRECTIONS):
            if d[2]:
                copies[d].wait_recv()
        low = jnp.sum(jnp.where(z_keep, hzr[f, 0], 0.0), axis=0, keepdims=True)
        high = jnp.sum(jnp.where(z_keep, hzr[f, 1], 0.0), axis=0, keepdims=True)
        low = jnp.sum(jnp.where(eye, low, 0.0), axis=1, keepdims=True)
        high = jnp.sum(jnp.where(eye, high, 0.0), axis=1, keepdims=True)
        return field + jnp.where(lane_id == 0, low, 0.0) + jnp.where(lane_id == 127, high, 0.0)

    def start_x(c):
        return (
            remote(vel.at[c, pl.ds(112, 16)], vhx.at[c, 0], vss.at[c, 0], vrs.at[c, 0], at_x(1)),
            remote(vel.at[c, pl.ds(0, 16)], vhx.at[c, 1], vss.at[c, 1], vrs.at[c, 1], at_x(-1)),
        )

    def mid_xy(c, copies):
        w = work.at[3 + c]
        w[...] = vel[c]
        copies[0].wait_recv()
        w[pl.ds(0, 16), :] = w[pl.ds(0, 16), :] + vhx[c, 0]
        copies[1].wait_recv()
        w[pl.ds(112, 16), :] = w[pl.ds(112, 16), :] + vhx[c, 1]
        both = w[pl.ds(7, 8, stride=16), :] + w[pl.ds(8, 8, stride=16), :]
        w[pl.ds(7, 8, stride=16), :] = both
        w[pl.ds(8, 8, stride=16), :] = both
        vys[c, 0] = w[pl.ds(15, 8, stride=16), :]
        vys[c, 1] = w[pl.ds(0, 8, stride=16), :]
        return (
            remote(vys.at[c, 0], vyr.at[c, 0], vss.at[c, 2], vrs.at[c, 2], at_y(1)),
            remote(vys.at[c, 1], vyr.at[c, 1], vss.at[c, 3], vrs.at[c, 3], at_y(-1)),
        )

    def mid_yz(c, copies):
        w = work.at[3 + c]
        copies[0].wait_recv()
        w[pl.ds(0, 8, stride=16), :] = w[pl.ds(0, 8, stride=16), :] + jnp.where(at_floor, 0.0, vyr[c, 0])
        copies[1].wait_recv()
        w[pl.ds(15, 8, stride=16), :] = w[pl.ds(15, 8, stride=16), :] + jnp.where(at_ceiling, 0.0, vyr[c, 1])
        field = w[...]
        vzs[c, 0] = jnp.sum(jnp.where(eye, field[:, 127:128], 0.0), axis=0, keepdims=True)
        vzs[c, 1] = jnp.sum(jnp.where(eye, field[:, 0:1], 0.0), axis=0, keepdims=True)
        out = (
            remote(vzs.at[c, 0], vzr.at[c, 0], vss.at[c, 4], vrs.at[c, 4], at_z(1)),
            remote(vzs.at[c, 1], vzr.at[c, 1], vss.at[c, 5], vrs.at[c, 5], at_z(-1)),
        )
        w[...] = (
            field
            + jnp.where(low_z, pltpu.roll(field, 1, 1), 0.0)
            + jnp.where(high_z, pltpu.roll(field, 127, 1), 0.0)
        )
        return out

    def end_z(c, copies):
        field = work[3 + c]
        copies[0].wait_recv()
        low = jnp.sum(jnp.where(eye, vzr[c, 0], 0.0), axis=1, keepdims=True)
        copies[1].wait_recv()
        high = jnp.sum(jnp.where(eye, vzr[c, 1], 0.0), axis=1, keepdims=True)
        field = field + jnp.where(lane_id == 0, low, 0.0) + jnp.where(lane_id == 127, high, 0.0)
        high = field.astype(BF16)
        vhi[pl.ds(128 * c, 128), :] = high
        vlo[pl.ds(128 * c, 128), :] = (field - high.astype(F32)).astype(BF16)

    table = deriv_table()

    def along_x(field, transposed):
        parts = [field[16 * i : 16 * i + 16, :] for i in range(8)]
        out = []
        for a in range(8):
            total = None
            for i in range(8):
                factor = table[i][a] if transposed else table[a][i]
                if factor == 0.0:
                    continue
                term = parts[i] * np.float32(factor)
                total = term if total is None else total + term
            out.append(total)
        return jnp.concatenate(out, axis=0)

    def gradients(field):
        return (
            along_x(field, False),
            jnp.dot(ky[...], field, precision=EXACT, preferred_element_type=F32),
            jnp.dot(field, kyt[...], precision=EXACT, preferred_element_type=F32),
        )

    def operator(field):
        dx, dy, dz = gradients(field)
        return (
            along_x(met[0] * dx, True)
            + jnp.dot(kyt[...], met[1] * dy, precision=EXACT, preferred_element_type=F32)
            + jnp.dot(met[2] * dz, ky[...], precision=EXACT, preferred_element_type=F32)
            + scr[...] * field
        ) * SCALE

    sendv[...] = jnp.zeros_like(sendv)
    loads["src"].wait()
    pack_faces(0, pack_planes(0, src[...]))
    pl.semaphore_wait(barrier, len(DIRECTIONS) + len(RING_Y))
    halo = {}
    send_halo(0, halo, True)
    send_halo(0, halo, False)
    loads["vel"].wait()
    cvx = [start_x(c) for c in range(3)]

    loads["coords"].wait()
    loads["owner"].wait()
    loads["elem"].wait()
    owned = (owner[...] == iota((GY, 512), 0)).astype(F32)
    tri = (iota((128, 128), 0) < iota((128, 128), 1)).astype(BF16)
    before = jnp.zeros((GY, 1), F32)
    rank = []
    for b in range(4):
        part = owned[:, 128 * b : 128 * b + 128]
        count = jnp.dot(part.astype(BF16), tri, preferred_element_type=F32) + before
        rank.append(jnp.sum(count * part, axis=0, keepdims=True))
        before = before + jnp.sum(part, axis=1, keepdims=True)
    rank = jnp.concatenate(rank, axis=1)
    slots = (rank.astype(jnp.int32) == iota((CAP, 512), 0)).astype(F32)
    data = jnp.concatenate(
        [coords[...], elem[...].astype(F32), jnp.zeros((4, 512), F32)], axis=0
    )
    lhs = jnp.concatenate([data * owned[g : g + 1, :] for g in range(GY)], axis=0)
    packed = lax.dot_general(
        lhs, slots, (((1,), (1,)), ((), ())), precision=EXACT, preferred_element_type=F32
    )
    for g in range(GY):
        sendp[g] = packed[8 * g : 8 * g + 8, :]

    to_owner = []
    for k in range(1, GY):
        peer = lax.rem(gy + k, GY)
        to_owner.append(
            remote(sendp.at[peer], recvp.at[gy], pss.at[0, k], prs.at[0, k], (gx, peer, gz))
        )
    recvp[gy] = sendp[gy]

    cvy = [mid_xy(c, cvx[c]) for c in range(3)]
    loads["ky"].wait()
    loads["kyt"].wait()
    loads["met"].wait()
    loads["scr"].wait()
    v0 = end_halo(0, halo)

    image0 = operator(v0)
    halo = start_halo(1, image0)
    cvz = [mid_yz(c, cvy[c]) for c in range(3)]
    v1 = end_halo(1, halo)
    image1 = operator(v1)
    halo = start_halo(2, image1)
    place_y = row_id % 16
    share_x = jnp.where((row_id < 16) | (row_id >= 112), 0.5, 1.0)
    edge_y = (place_y % 8 == 0) | (place_y % 8 == 7)
    wall = ((place_y == 0) & at_floor) | ((place_y == 15) & at_ceiling)
    share_y = jnp.where(edge_y & jnp.logical_not(wall), 0.5, 1.0)
    share_z = jnp.where((lane_in == 0) | (lane_in == 7), 0.5, 1.0)
    weight = share_x * share_y * share_z
    early = jnp.concatenate(
        [
            jnp.sum(value, axis=0, keepdims=True)
            for value in (weight * v0 * v0, v0 * image0, weight * v1 * v1, v1 * image1)
        ],
        axis=0,
    )
    for c in range(3):
        end_z(c, cvz[c])

    loads["lsc"].wait()
    for copy in to_owner:
        copy.wait_recv()
    points = gll_points()
    node = iota((8, 128), 0)

    def basis(coord):
        product = lsc[...]
        for m in range(8):
            product = product * jnp.where(node == m, 1.0, coord - np.float32(points[m]))
        return product

    def sample_two(step, carry):
        low_parts, high_parts, weights = [], [], []
        for half in range(2):
            block = recvp[2 * step + half]
            element = block[3:4, :].astype(jnp.int32)
            bx, by, bz = (basis(block[d : d + 1, :]) for d in range(3))
            element_y = element // 16
            element_z = element % 16
            wide = jnp.concatenate(
                [jnp.where(element_z == e, bz, 0.0) for e in range(16)], axis=0
            )
            high = wide.astype(BF16)
            high_parts.append(high)
            low_parts.append((wide - high.astype(F32)).astype(BF16))
            tall = jnp.concatenate(
                [jnp.where(element_y == e, by, 0.0) for e in range(2)], axis=0
            )
            weights.append(
                jnp.concatenate([bx[i : i + 1, :] * tall for i in range(8)], axis=0)
            )
        high = jnp.concatenate(high_parts, axis=1)
        low = jnp.concatenate(low_parts, axis=1)
        for c in range(3):
            vh = vhi[pl.ds(128 * c, 128), :]
            partial = (
                jnp.dot(vh, high, preferred_element_type=F32)
                + jnp.dot(vh, low, preferred_element_type=F32)
                + jnp.dot(vlo[pl.ds(128 * c, 128), :], high, preferred_element_type=F32)
            )
            for half in range(2):
                sendv[2 * step + half, pl.ds(c, 1), :] = jnp.sum(
                    partial[:, 128 * half : 128 * half + 128] * weights[half], axis=0, keepdims=True
                )
        return carry

    lax.fori_loop(0, GY // 2, sample_two, 0)

    to_home = []
    for k in range(1, GY):
        peer = lax.rem(gy + k, GY)
        to_home.append(
            remote(sendv.at[peer], recvv.at[gy], pss.at[1, k], prs.at[1, k], (gx, peer, gz))
        )
    recvv[gy] = sendv[gy]
    v2 = end_halo(2, halo)

    dx, dy, dz = gradients(v2)
    rows = jnp.concatenate(
        [
            early,
            jnp.sum(weight * v2 * v2, axis=0, keepdims=True),
            jnp.sum(
                (met[0] * dx * dx + met[1] * dy * dy + met[2] * dz * dz + scr[...] * v2 * v2) * SCALE,
                axis=0,
                keepdims=True,
            ),
            jnp.zeros((2, 128), F32),
        ],
        axis=0,
    )
    total = jnp.sum(rows, axis=1, keepdims=True)
    row = jnp.sum(
        jnp.where(iota((8, 128), 0) == iota((8, 128), 1), total, 0.0), axis=0, keepdims=True
    )

    msg[0] = row
    here = gx * GZ + gz
    rxz[here] = row
    copies = []
    for i in range(GX):
        for k in range(GZ):
            if i or k:
                n = i * GZ + k
                device = (lax.rem(gx + i, GX), gy, lax.rem(gz + k, GZ))
                copies.append(remote(msg.at[0], rxz.at[here], ass.at[n], ars.at[n], device))
    for copy in copies:
        copy.wait_recv()
    row = jnp.sum(rxz[...], axis=0)
    msg[1] = row
    ry[gy] = row
    copies = []
    for k in range(1, GY):
        n = GX * GZ + k
        copies.append(remote(msg.at[1], ry.at[gy], ass.at[n], ars.at[n], at_y(k)))

    for copy in to_home:
        copy.wait_recv()
    back = jnp.concatenate([recvv[g] for g in range(GY)], axis=0)
    spread = jnp.dot(back, slots, precision=EXACT, preferred_element_type=F32)
    velocity = jnp.zeros((8, 512), F32)
    for g in range(GY):
        velocity = velocity + spread[8 * g : 8 * g + 8, :] * owned[g : g + 1, :]
    pv_out[...] = velocity[0:3, :]

    for copy in copies:
        copy.wait_recv()
    row = jnp.sum(ry[...], axis=0)

    lane = iota((1, 128), 1)
    m = [jnp.sum(jnp.where(lane == k, row, 0.0), axis=1, keepdims=True) for k in range(6)]

    def form(coefficients, shift):
        total = None
        for i, left in enumerate(coefficients):
            for j, right in enumerate(coefficients):
                term = left * right * m[i + j + shift]
                total = term if total is None else total + term
        return total

    one = jnp.ones_like(m[0])
    rr = m[0]
    direction = [one]
    residual = [one]
    solution_row = [jnp.zeros_like(one)] * 3
    for step in range(3):
        alpha = rr / form(direction, 1)
        for i, value in enumerate(direction):
            solution_row[i] = solution_row[i] + alpha * value
        if step == 2:
            break
        residual = residual + [jnp.zeros_like(one)]
        for i, value in enumerate(direction):
            residual[i + 1] = residual[i + 1] - alpha * value
        new = form(residual, 0)
        beta = new / rr
        direction = [
            value + beta * direction[i] if i < len(direction) else value
            for i, value in enumerate(residual)
        ]
        rr = new
    p_out[...] = (solution_row[0] * v0 + solution_row[1] * v1 + solution_row[2] * v2) * SCALE

    for copy in sends:
        copy.wait_send()


def body(vel, src, met, scr, coords, owner, elem):
    table = np.array(deriv_table(), np.float32)
    kron = np.kron(np.eye(16, dtype=np.float32), table)
    lsc = np.repeat(np.array(lagrange_scale(), np.float32)[:, None], 128, axis=1)
    operands = (
        vel.reshape(3, 128, 128),
        src.reshape(128, 128),
        met.reshape(3, 128, 128),
        scr.reshape(128, 128),
        coords,
        owner.reshape(1, 512),
        elem.reshape(1, 512),
        jnp.asarray(kron),
        jnp.asarray(kron.T),
        jnp.asarray(lsc),
    )
    anywhere = pl.BlockSpec(memory_space=pl.ANY)
    vmem = pl.BlockSpec(memory_space=pltpu.VMEM)
    dma = pltpu.SemaphoreType.DMA
    pressure, velocity = pl.pallas_call(
        kernel,
        out_shape=(
            pltpu.VMEM((128, 128), F32),
            pltpu.VMEM((3, 512), F32),
        ),
        in_specs=[anywhere] * len(operands),
        out_specs=(vmem, vmem),
        scratch_shapes=[pltpu.VMEM(x.shape, x.dtype) for x in operands]
        + [
            dma((len(operands),)),
            pltpu.VMEM((6, 128, 128), F32),
            pltpu.VMEM((3, 2, 16, 128), F32),
            pltpu.VMEM((3, 2, 16, 128), F32),
            pltpu.VMEM((3, 2, 8, 128), F32),
            pltpu.VMEM((3, 2, 8, 128), F32),
            pltpu.VMEM((3, 4, 1, 128), F32),
            pltpu.VMEM((3, 4, 1, 128), F32),
            pltpu.VMEM((3, 9, 2, 128), F32),
            pltpu.VMEM((3, 2, 16, 128), F32),
            dma((3, 26)),
            dma((3, 26)),
            pltpu.VMEM((3, 2, 16, 128), F32),
            pltpu.VMEM((3, 2, 8, 128), F32),
            pltpu.VMEM((3, 2, 8, 128), F32),
            pltpu.VMEM((3, 2, 1, 128), F32),
            pltpu.VMEM((3, 2, 1, 128), F32),
            dma((3, 6)),
            dma((3, 6)),
            pltpu.VMEM((2, 1, 128), F32),
            pltpu.VMEM((GX * GZ, 1, 128), F32),
            pltpu.VMEM((GY, 1, 128), F32),
            dma((GX * GZ + GY,)),
            dma((GX * GZ + GY,)),
            pltpu.VMEM((GY, 8, 128), F32),
            pltpu.VMEM((GY, 8, 128), F32),
            pltpu.VMEM((GY, 8, 128), F32),
            pltpu.VMEM((GY, 8, 128), F32),
            dma((2, GY)),
            dma((2, GY)),
            pltpu.VMEM((384, 128), BF16),
            pltpu.VMEM((384, 128), BF16),
        ],
        compiler_params=pltpu.CompilerParams(collective_id=0, has_side_effects=True),
        name="step",
    )(*operands)
    return pressure.reshape(8, 16, 128), velocity


def solution(mesh):
    in_specs = (
        P(None, "gx", "gy", "gz"),
        P("gx", "gy", "gz"),
        P(None, "gx", "gy", "gz"),
        P("gx", "gy", "gz"),
        P(None, ("gx", "gy", "gz")),
        P(("gx", "gy", "gz"), None),
        P(("gx", "gy", "gz")),
    )
    out_specs = (P("gx", "gy", "gz"), P(None, ("gx", "gy", "gz")))
    return jax.shard_map(body, mesh=mesh, in_specs=in_specs, out_specs=out_specs, check_vma=False)
```

```python
import itertools

import jax
import jax.numpy as jnp
import numpy as np
from jax import lax
from jax.experimental import pallas as pl
from jax.experimental.pallas import tpu as pltpu
from jax.sharding import PartitionSpec as P

MESH = pl.DeviceIdType.MESH
F32 = jnp.float32
BF16 = jnp.bfloat16
EXACT = lax.Precision.HIGHEST
SCALE = 1.0 / 64.0
GX, GY, GZ = 4, 16, 8
CAP = 128


def gll_points():
    return [
        -1.0,
        -0.8717401485096066,
        -0.5917001814331423,
        -0.2092992179024789,
        0.2092992179024789,
        0.5917001814331423,
        0.8717401485096066,
        1.0,
    ]


def legendre_seven(point):
    before, current = (1.0, point)
    for order in range(1, 7):
        before, current = (
            current,
            ((2 * order + 1) * point * current - order * before) / (order + 1),
        )
    return current


def deriv_table():
    points = gll_points()
    legendre = [legendre_seven(value) for value in points]
    derivative = [[0.0] * 8 for row in range(8)]
    for i in range(8):
        for j in range(8):
            if i != j:
                derivative[i][j] = legendre[i] / legendre[j] / (points[i] - points[j])
    derivative[0][0] = -14.0
    derivative[7][7] = 14.0
    return derivative


def lagrange_scale():
    points = gll_points()
    scale = []
    for i in range(8):
        product = 1.0
        for m in range(8):
            if m != i:
                product *= points[i] - points[m]
        scale.append(1.0 / product)
    return scale


def iota(shape, dim):
    return lax.broadcasted_iota(jnp.int32, shape, dim)


DIRECTIONS = sorted(
    (d for d in itertools.product((-1, 0, 1), repeat=3) if any(d)),
    key=lambda d: -sum(abs(v) for v in d),
)
SENT_ROWS = 3 * 70 + 150 + 31 + 15 + 2 * 120
RING_Y = [k for k in range(2, GY - 1)]


def kernel(
    vel_in, src_in, met_in, scr_in, coords_in, owner_in, elem_in, ky_in, kyt_in, lsc_in,
    p_out, pv_out,
    vel, src, met, scr, coords, owner, elem, ky, kyt, lsc, load_sem,
    work, hxs, hx, hys, hyr, hes, her, hzs, hzr, halo_sem,
    vhx, vys, vyr, vzs, vzr, velocity_sem,
    msg, rxz, ry, sum_sem,
    sendp, recvp, sendv, recvv, particle_sem, vhi, vlo,
    send_sem, measure,
):
    gx, gy, gz = lax.axis_index("gx"), lax.axis_index("gy"), lax.axis_index("gz")

    def at_x(k):
        return (lax.rem(gx + (k + GX), GX), gy, gz)

    def at_y(k):
        return (gx, lax.rem(gy + (k + GY), GY), gz)

    def at_z(k):
        return (gx, gy, lax.rem(gz + (k + GZ), GZ))

    def near(d):
        return (
            lax.rem(gx + (d[0] + GX), GX),
            lax.rem(gy + (d[1] + GY), GY),
            lax.rem(gz + (d[2] + GZ), GZ),
        )

    barrier = pltpu.get_barrier_semaphore()
    for d in DIRECTIONS:
        pl.semaphore_signal(barrier, inc=1, device_id=near(d), device_id_type=MESH)
    for k in RING_Y:
        pl.semaphore_signal(barrier, inc=1, device_id=at_y(k), device_id_type=MESH)

    loads = {}
    for i, (name, source, target) in enumerate((
        ("src", src_in, src), ("vel", vel_in, vel), ("ky", ky_in, ky), ("kyt", kyt_in, kyt),
        ("met", met_in, met), ("scr", scr_in, scr), ("coords", coords_in, coords),
        ("owner", owner_in, owner), ("elem", elem_in, elem), ("lsc", lsc_in, lsc),
    )):
        loads[name] = pltpu.make_async_copy(source, target, load_sem.at[i])
        loads[name].start()

    sent_rows = []

    def remote(source, target, sem, device, rows):
        pltpu.make_async_remote_copy(
            src_ref=source,
            dst_ref=target,
            send_sem=send_sem.at[0],
            recv_sem=sem,
            device_id=device,
            device_id_type=MESH,
        ).start()
        sent_rows.append(rows)

    def wait_rows(sem, rows):
        piece = measure.at[pl.ds(0, rows)]
        pltpu.make_async_copy(piece, piece, sem).wait()

    row_id = iota((128, 128), 0)
    lane_id = iota((128, 128), 1)
    eye = row_id == lane_id
    lane_in = lane_id % 8
    low_z = (lane_in == 0) & (lane_id > 0)
    high_z = (lane_in == 7) & (lane_id < 127)
    at_floor = gy == 0
    at_ceiling = gy == GY - 1

    def source_mask():
        index = iota((16, 128), 0)
        lane = iota((16, 128), 1)
        from_x, from_y = index // 3 - 1, index % 3 - 1
        in_x, in_y = lane // 16, lane % 16
        keep = (index < 9) & jnp.logical_not((from_y == -1) & at_floor)
        keep = keep & jnp.logical_not((from_y == 1) & at_ceiling)
        keep = keep & ((from_x == 0) | ((from_x == -1) & (in_x == 0)) | ((from_x == 1) & (in_x == 7)))
        return keep & ((from_y == 0) | ((from_y == -1) & (in_y == 0)) | ((from_y == 1) & (in_y == 15)))

    z_keep = source_mask()

    def pack_planes(f, field):
        w = work.at[f]
        w[...] = field
        both = w[pl.ds(7, 8, stride=16), :] + w[pl.ds(8, 8, stride=16), :]
        w[pl.ds(7, 8, stride=16), :] = both
        w[pl.ds(8, 8, stride=16), :] = both
        field = w[...]
        pair = jnp.concatenate(
            [
                jnp.sum(jnp.where(eye, field[:, 127:128], 0.0), axis=0, keepdims=True),
                jnp.sum(jnp.where(eye, field[:, 0:1], 0.0), axis=0, keepdims=True),
            ],
            axis=0,
        )
        for dx in (-1, 0, 1):
            for dy in (-1, 0, 1):
                shift = (16 * dx - 15 * dy) % 128
                hzs[f, (1 - dx) * 3 + (1 - dy)] = pltpu.roll(pair, shift, 1) if shift else pair
        return field

    def pack_faces(f, field):
        w = work.at[f]
        field = (
            field
            + jnp.where(low_z, pltpu.roll(field, 1, 1), 0.0)
            + jnp.where(high_z, pltpu.roll(field, 127, 1), 0.0)
        )
        w[...] = field
        for d in DIRECTIONS:
            if d[2] == 0 and d[0] and d[1]:
                row = (112 if d[0] == 1 else 0) + (15 if d[1] == 1 else 0)
                hes[f, (1 - d[0]) + (1 - d[1]) // 2] = field[row : row + 1, :]
        hxs[f, 0] = field[112:128, :]
        hxs[f, 1] = field[0:16, :]
        hys[f, 0] = w[pl.ds(15, 8, stride=16), :]
        hys[f, 1] = w[pl.ds(0, 8, stride=16), :]

    def send_halo(f, planes):
        for d in DIRECTIONS:
            if planes != (d[2] != 0):
                continue
            rows = 1
            if d[2]:
                j, side = (1 - d[0]) * 3 + (1 - d[1]), (1 - d[2]) // 2
                source, target = hzs.at[f, j, pl.ds(side, 1)], hzr.at[f, side, pl.ds(j, 1)]
            elif d[0] and d[1]:
                e = (1 - d[0]) + (1 - d[1]) // 2
                source, target = hes.at[f, e], her.at[f, e]
            elif d[0]:
                source, target = hxs.at[f, (1 - d[0]) // 2], hx.at[f, (1 - d[0]) // 2]
                rows = 16
            else:
                source, target = hys.at[f, (1 - d[1]) // 2], hyr.at[f, (1 - d[1]) // 2]
                rows = 8
            remote(source, target, halo_sem.at[f, 1 if planes else 0], near(d), rows)

    def start_halo(f, field):
        field = pack_planes(f, field)
        send_halo(f, True)
        pack_faces(f, field)
        send_halo(f, False)

    def end_halo(f):
        w = work.at[f]
        wait_rows(halo_sem.at[f, 0], 52)
        w[pl.ds(0, 8, stride=16), :] = w[pl.ds(0, 8, stride=16), :] + jnp.where(at_floor, 0.0, hyr[f, 0])
        w[pl.ds(15, 8, stride=16), :] = w[pl.ds(15, 8, stride=16), :] + jnp.where(at_ceiling, 0.0, hyr[f, 1])
        w[pl.ds(0, 16), :] = w[pl.ds(0, 16), :] + hx[f, 0]
        w[pl.ds(112, 16), :] = w[pl.ds(112, 16), :] + hx[f, 1]
        for d in DIRECTIONS:
            if d[2] == 0 and d[0] and d[1]:
                e = (1 - d[0]) + (1 - d[1]) // 2
                row = (0 if d[0] == 1 else 112) + (0 if d[1] == 1 else 15)
                cut = at_floor if d[1] == 1 else at_ceiling
                w[pl.ds(row, 1), :] = w[pl.ds(row, 1), :] + jnp.where(cut, 0.0, her[f, e])
        field = w[...]
        wait_rows(halo_sem.at[f, 1], 18)
        low = jnp.sum(jnp.where(z_keep, hzr[f, 0], 0.0), axis=0, keepdims=True)
        high = jnp.sum(jnp.where(z_keep, hzr[f, 1], 0.0), axis=0, keepdims=True)
        low = jnp.sum(jnp.where(eye, low, 0.0), axis=1, keepdims=True)
        high = jnp.sum(jnp.where(eye, high, 0.0), axis=1, keepdims=True)
        return field + jnp.where(lane_id == 0, low, 0.0) + jnp.where(lane_id == 127, high, 0.0)

    def start_x():
        for c in range(3):
            remote(vel.at[c, pl.ds(112, 16)], vhx.at[c, 0], velocity_sem.at[0], at_x(1), 16)
            remote(vel.at[c, pl.ds(0, 16)], vhx.at[c, 1], velocity_sem.at[0], at_x(-1), 16)

    def mid_xy():
        wait_rows(velocity_sem.at[0], 96)
        for c in range(3):
            w = work.at[3 + c]
            w[...] = vel[c]
            w[pl.ds(0, 16), :] = w[pl.ds(0, 16), :] + vhx[c, 0]
            w[pl.ds(112, 16), :] = w[pl.ds(112, 16), :] + vhx[c, 1]
            both = w[pl.ds(7, 8, stride=16), :] + w[pl.ds(8, 8, stride=16), :]
            w[pl.ds(7, 8, stride=16), :] = both
            w[pl.ds(8, 8, stride=16), :] = both
            vys[c, 0] = w[pl.ds(15, 8, stride=16), :]
            vys[c, 1] = w[pl.ds(0, 8, stride=16), :]
            remote(vys.at[c, 0], vyr.at[c, 0], velocity_sem.at[1], at_y(1), 8)
            remote(vys.at[c, 1], vyr.at[c, 1], velocity_sem.at[1], at_y(-1), 8)

    def mid_yz():
        wait_rows(velocity_sem.at[1], 48)
        for c in range(3):
            w = work.at[3 + c]
            w[pl.ds(0, 8, stride=16), :] = w[pl.ds(0, 8, stride=16), :] + jnp.where(at_floor, 0.0, vyr[c, 0])
            w[pl.ds(15, 8, stride=16), :] = w[pl.ds(15, 8, stride=16), :] + jnp.where(at_ceiling, 0.0, vyr[c, 1])
            field = w[...]
            vzs[c, 0] = jnp.sum(jnp.where(eye, field[:, 127:128], 0.0), axis=0, keepdims=True)
            vzs[c, 1] = jnp.sum(jnp.where(eye, field[:, 0:1], 0.0), axis=0, keepdims=True)
            remote(vzs.at[c, 0], vzr.at[c, 0], velocity_sem.at[2], at_z(1), 1)
            remote(vzs.at[c, 1], vzr.at[c, 1], velocity_sem.at[2], at_z(-1), 1)
            w[...] = (
                field
                + jnp.where(low_z, pltpu.roll(field, 1, 1), 0.0)
                + jnp.where(high_z, pltpu.roll(field, 127, 1), 0.0)
            )

    def end_z():
        wait_rows(velocity_sem.at[2], 6)
        for c in range(3):
            field = work[3 + c]
            low = jnp.sum(jnp.where(eye, vzr[c, 0], 0.0), axis=1, keepdims=True)
            high = jnp.sum(jnp.where(eye, vzr[c, 1], 0.0), axis=1, keepdims=True)
            field = field + jnp.where(lane_id == 0, low, 0.0) + jnp.where(lane_id == 127, high, 0.0)
            high = field.astype(BF16)
            vhi[pl.ds(128 * c, 128), :] = high
            vlo[pl.ds(128 * c, 128), :] = (field - high.astype(F32)).astype(BF16)

    table = deriv_table()

    def along_x(field, transposed):
        parts = [field[16 * i : 16 * i + 16, :] for i in range(8)]
        out = []
        for a in range(8):
            total = None
            for i in range(8):
                factor = table[i][a] if transposed else table[a][i]
                if factor == 0.0:
                    continue
                term = parts[i] * np.float32(factor)
                total = term if total is None else total + term
            out.append(total)
        return jnp.concatenate(out, axis=0)

    def gradients(field):
        return (
            along_x(field, False),
            jnp.dot(ky[...], field, precision=EXACT, preferred_element_type=F32),
            jnp.dot(field, kyt[...], precision=EXACT, preferred_element_type=F32),
        )

    def operator(field):
        dx, dy, dz = gradients(field)
        return (
            along_x(met[0] * dx, True)
            + jnp.dot(kyt[...], met[1] * dy, precision=EXACT, preferred_element_type=F32)
            + jnp.dot(met[2] * dz, ky[...], precision=EXACT, preferred_element_type=F32)
            + scr[...] * field
        ) * SCALE

    sendv[...] = jnp.zeros_like(sendv)
    loads["src"].wait()
    pack_faces(0, pack_planes(0, src[...]))
    pl.semaphore_wait(barrier, len(DIRECTIONS) + len(RING_Y))
    send_halo(0, True)
    send_halo(0, False)
    loads["vel"].wait()
    start_x()

    loads["coords"].wait()
    loads["owner"].wait()
    loads["elem"].wait()
    owned = (owner[...] == iota((GY, 512), 0)).astype(F32)
    tri = (iota((128, 128), 0) < iota((128, 128), 1)).astype(BF16)
    before = jnp.zeros((GY, 1), F32)
    rank = []
    for b in range(4):
        part = owned[:, 128 * b : 128 * b + 128]
        count = jnp.dot(part.astype(BF16), tri, preferred_element_type=F32) + before
        rank.append(jnp.sum(count * part, axis=0, keepdims=True))
        before = before + jnp.sum(part, axis=1, keepdims=True)
    rank = jnp.concatenate(rank, axis=1)
    slots = (rank.astype(jnp.int32) == iota((CAP, 512), 0)).astype(F32)
    data = jnp.concatenate(
        [coords[...], elem[...].astype(F32), jnp.zeros((4, 512), F32)], axis=0
    )
    lhs = jnp.concatenate([data * owned[g : g + 1, :] for g in range(GY)], axis=0)
    packed = lax.dot_general(
        lhs, slots, (((1,), (1,)), ((), ())), precision=EXACT, preferred_element_type=F32
    )
    for g in range(GY):
        sendp[g] = packed[8 * g : 8 * g + 8, :]

    for k in range(1, GY):
        peer = lax.rem(gy + k, GY)
        remote(sendp.at[peer], recvp.at[gy], particle_sem.at[0], (gx, peer, gz), 8)
    recvp[gy] = sendp[gy]

    mid_xy()
    loads["ky"].wait()
    loads["kyt"].wait()
    loads["met"].wait()
    loads["scr"].wait()
    v0 = end_halo(0)

    image0 = operator(v0)
    start_halo(1, image0)
    mid_yz()
    v1 = end_halo(1)
    image1 = operator(v1)
    start_halo(2, image1)
    place_y = row_id % 16
    share_x = jnp.where((row_id < 16) | (row_id >= 112), 0.5, 1.0)
    edge_y = (place_y % 8 == 0) | (place_y % 8 == 7)
    wall = ((place_y == 0) & at_floor) | ((place_y == 15) & at_ceiling)
    share_y = jnp.where(edge_y & jnp.logical_not(wall), 0.5, 1.0)
    share_z = jnp.where((lane_in == 0) | (lane_in == 7), 0.5, 1.0)
    weight = share_x * share_y * share_z
    early = jnp.concatenate(
        [
            jnp.sum(value, axis=0, keepdims=True)
            for value in (weight * v0 * v0, v0 * image0, weight * v1 * v1, v1 * image1)
        ],
        axis=0,
    )
    end_z()

    loads["lsc"].wait()
    wait_rows(particle_sem.at[0], 8 * (GY - 1))
    points = gll_points()
    node = iota((8, 128), 0)

    def basis(coord):
        product = lsc[...]
        for m in range(8):
            product = product * jnp.where(node == m, 1.0, coord - np.float32(points[m]))
        return product

    def sample_two(step, carry):
        low_parts, high_parts, weights = [], [], []
        for half in range(2):
            block = recvp[2 * step + half]
            element = block[3:4, :].astype(jnp.int32)
            bx, by, bz = (basis(block[d : d + 1, :]) for d in range(3))
            element_y = element // 16
            element_z = element % 16
            wide = jnp.concatenate(
                [jnp.where(element_z == e, bz, 0.0) for e in range(16)], axis=0
            )
            high = wide.astype(BF16)
            high_parts.append(high)
            low_parts.append((wide - high.astype(F32)).astype(BF16))
            tall = jnp.concatenate(
                [jnp.where(element_y == e, by, 0.0) for e in range(2)], axis=0
            )
            weights.append(
                jnp.concatenate([bx[i : i + 1, :] * tall for i in range(8)], axis=0)
            )
        high = jnp.concatenate(high_parts, axis=1)
        low = jnp.concatenate(low_parts, axis=1)
        for c in range(3):
            vh = vhi[pl.ds(128 * c, 128), :]
            partial = (
                jnp.dot(vh, high, preferred_element_type=F32)
                + jnp.dot(vh, low, preferred_element_type=F32)
                + jnp.dot(vlo[pl.ds(128 * c, 128), :], high, preferred_element_type=F32)
            )
            for half in range(2):
                sendv[2 * step + half, pl.ds(c, 1), :] = jnp.sum(
                    partial[:, 128 * half : 128 * half + 128] * weights[half], axis=0, keepdims=True
                )
        return carry

    lax.fori_loop(0, GY // 2, sample_two, 0)

    for k in range(1, GY):
        peer = lax.rem(gy + k, GY)
        remote(sendv.at[peer], recvv.at[gy], particle_sem.at[1], (gx, peer, gz), 8)
    recvv[gy] = sendv[gy]
    v2 = end_halo(2)

    dx, dy, dz = gradients(v2)
    rows = jnp.concatenate(
        [
            early,
            jnp.sum(weight * v2 * v2, axis=0, keepdims=True),
            jnp.sum(
                (met[0] * dx * dx + met[1] * dy * dy + met[2] * dz * dz + scr[...] * v2 * v2) * SCALE,
                axis=0,
                keepdims=True,
            ),
            jnp.zeros((2, 128), F32),
        ],
        axis=0,
    )
    total = jnp.sum(rows, axis=1, keepdims=True)
    row = jnp.sum(
        jnp.where(iota((8, 128), 0) == iota((8, 128), 1), total, 0.0), axis=0, keepdims=True
    )

    msg[0] = row
    here = gx * GZ + gz
    rxz[here] = row
    for i in range(GX):
        for k in range(GZ):
            if i or k:
                device = (lax.rem(gx + i, GX), gy, lax.rem(gz + k, GZ))
                remote(msg.at[0], rxz.at[here], sum_sem.at[0], device, 1)
    wait_rows(sum_sem.at[0], GX * GZ - 1)
    row = jnp.sum(rxz[...], axis=0)
    msg[1] = row
    ry[gy] = row
    for k in range(1, GY):
        remote(msg.at[1], ry.at[gy], sum_sem.at[1], at_y(k), 1)

    wait_rows(particle_sem.at[1], 8 * (GY - 1))
    back = jnp.concatenate([recvv[g] for g in range(GY)], axis=0)
    spread = jnp.dot(back, slots, precision=EXACT, preferred_element_type=F32)
    velocity = jnp.zeros((8, 512), F32)
    for g in range(GY):
        velocity = velocity + spread[8 * g : 8 * g + 8, :] * owned[g : g + 1, :]
    pv_out[...] = velocity[0:3, :]

    wait_rows(sum_sem.at[1], GY - 1)
    row = jnp.sum(ry[...], axis=0)

    lane = iota((1, 128), 1)
    m = [jnp.sum(jnp.where(lane == k, row, 0.0), axis=1, keepdims=True) for k in range(6)]

    def form(coefficients, shift):
        total = None
        for i, left in enumerate(coefficients):
            for j, right in enumerate(coefficients):
                term = left * right * m[i + j + shift]
                total = term if total is None else total + term
        return total

    one = jnp.ones_like(m[0])
    rr = m[0]
    direction = [one]
    residual = [one]
    solution_row = [jnp.zeros_like(one)] * 3
    for step in range(3):
        alpha = rr / form(direction, 1)
        for i, value in enumerate(direction):
            solution_row[i] = solution_row[i] + alpha * value
        if step == 2:
            break
        residual = residual + [jnp.zeros_like(one)]
        for i, value in enumerate(direction):
            residual[i + 1] = residual[i + 1] - alpha * value
        new = form(residual, 0)
        beta = new / rr
        direction = [
            value + beta * direction[i] if i < len(direction) else value
            for i, value in enumerate(residual)
        ]
        rr = new
    p_out[...] = (solution_row[0] * v0 + solution_row[1] * v1 + solution_row[2] * v2) * SCALE

    wait_rows(send_sem.at[0], sum(sent_rows))
    assert sum(sent_rows) == SENT_ROWS


def body(vel, src, met, scr, coords, owner, elem):
    table = np.array(deriv_table(), np.float32)
    kron = np.kron(np.eye(16, dtype=np.float32), table)
    lsc = np.repeat(np.array(lagrange_scale(), np.float32)[:, None], 128, axis=1)
    operands = (
        vel.reshape(3, 128, 128),
        src.reshape(128, 128),
        met.reshape(3, 128, 128),
        scr.reshape(128, 128),
        coords,
        owner.reshape(1, 512),
        elem.reshape(1, 512),
        jnp.asarray(kron),
        jnp.asarray(kron.T),
        jnp.asarray(lsc),
    )
    anywhere = pl.BlockSpec(memory_space=pl.ANY)
    vmem = pl.BlockSpec(memory_space=pltpu.VMEM)
    dma = pltpu.SemaphoreType.DMA
    pressure, velocity = pl.pallas_call(
        kernel,
        out_shape=(
            pltpu.VMEM((128, 128), F32),
            pltpu.VMEM((3, 512), F32),
        ),
        in_specs=[anywhere] * len(operands),
        out_specs=(vmem, vmem),
        scratch_shapes=[pltpu.VMEM(x.shape, x.dtype) for x in operands]
        + [
            dma((len(operands),)),
            pltpu.VMEM((6, 128, 128), F32),
            pltpu.VMEM((3, 2, 16, 128), F32),
            pltpu.VMEM((3, 2, 16, 128), F32),
            pltpu.VMEM((3, 2, 8, 128), F32),
            pltpu.VMEM((3, 2, 8, 128), F32),
            pltpu.VMEM((3, 4, 1, 128), F32),
            pltpu.VMEM((3, 4, 1, 128), F32),
            pltpu.VMEM((3, 9, 2, 128), F32),
            pltpu.VMEM((3, 2, 16, 128), F32),
            dma((3, 2)),
            pltpu.VMEM((3, 2, 16, 128), F32),
            pltpu.VMEM((3, 2, 8, 128), F32),
            pltpu.VMEM((3, 2, 8, 128), F32),
            pltpu.VMEM((3, 2, 1, 128), F32),
            pltpu.VMEM((3, 2, 1, 128), F32),
            dma((3,)),
            pltpu.VMEM((2, 1, 128), F32),
            pltpu.VMEM((GX * GZ, 1, 128), F32),
            pltpu.VMEM((GY, 1, 128), F32),
            dma((2,)),
            pltpu.VMEM((GY, 8, 128), F32),
            pltpu.VMEM((GY, 8, 128), F32),
            pltpu.VMEM((GY, 8, 128), F32),
            pltpu.VMEM((GY, 8, 128), F32),
            dma((2,)),
            pltpu.VMEM((384, 128), BF16),
            pltpu.VMEM((384, 128), BF16),
            dma((1,)),
            pltpu.VMEM((SENT_ROWS, 1, 128), F32),
        ],
        compiler_params=pltpu.CompilerParams(collective_id=0, has_side_effects=True),
        name="step",
    )(*operands)
    return pressure.reshape(8, 16, 128), velocity


def solution(mesh):
    in_specs = (
        P(None, "gx", "gy", "gz"),
        P("gx", "gy", "gz"),
        P(None, "gx", "gy", "gz"),
        P("gx", "gy", "gz"),
        P(None, ("gx", "gy", "gz")),
        P(("gx", "gy", "gz"), None),
        P(("gx", "gy", "gz")),
    )
    out_specs = (P("gx", "gy", "gz"), P(None, ("gx", "gy", "gz")))
    return jax.shard_map(body, mesh=mesh, in_specs=in_specs, out_specs=out_specs, check_vma=False)
```

```python
import itertools

import jax
import jax.numpy as jnp
import numpy as np
from jax import lax
from jax.experimental import pallas as pl
from jax.experimental.pallas import tpu as pltpu
from jax.sharding import PartitionSpec as P

MESH = pl.DeviceIdType.MESH
F32 = jnp.float32
BF16 = jnp.bfloat16
EXACT = lax.Precision.HIGHEST
SCALE = 1.0 / 64.0
GX, GY, GZ = 4, 16, 8
CAP = 128


def gll_points():
    return [
        -1.0,
        -0.8717401485096066,
        -0.5917001814331423,
        -0.2092992179024789,
        0.2092992179024789,
        0.5917001814331423,
        0.8717401485096066,
        1.0,
    ]


def legendre_seven(point):
    before, current = (1.0, point)
    for order in range(1, 7):
        before, current = (
            current,
            ((2 * order + 1) * point * current - order * before) / (order + 1),
        )
    return current


def deriv_table():
    points = gll_points()
    legendre = [legendre_seven(value) for value in points]
    derivative = [[0.0] * 8 for row in range(8)]
    for i in range(8):
        for j in range(8):
            if i != j:
                derivative[i][j] = legendre[i] / legendre[j] / (points[i] - points[j])
    derivative[0][0] = -14.0
    derivative[7][7] = 14.0
    return derivative


def lagrange_scale():
    points = gll_points()
    scale = []
    for i in range(8):
        product = 1.0
        for m in range(8):
            if m != i:
                product *= points[i] - points[m]
        scale.append(1.0 / product)
    return scale


def iota(shape, dim):
    return lax.broadcasted_iota(jnp.int32, shape, dim)


DIRECTIONS = sorted(
    (d for d in itertools.product((-1, 0, 1), repeat=3) if any(d)),
    key=lambda d: -sum(abs(v) for v in d),
)
SENT_ROWS = 3 * 70 + 150 + 31 + 15 + 2 * 120
FAR_XZ = sorted(
    ((i, k) for i in range(GX) for k in range(GZ) if i or k),
    key=lambda p: -min(p[0], GX - p[0]) - min(p[1], GZ - p[1]),
)
FAR_Y = sorted(range(1, GY), key=lambda k: -min(k, GY - k))
RING_Y = [k for k in range(2, GY - 1)]


def tree(values):
    while len(values) > 1:
        values = [a + b for a, b in zip(values[0::2], values[1::2])]
    return values[0]


def kernel(
    vel_in, src_in, met_in, scr_in, coords_in, owner_in, elem_in, ky_in, kyt_in, lsc_in,
    p_out, pv_out,
    vel, src, met, scr, coords, owner, elem, ky, kyt, lsc, load_sem,
    work, hxs, hx, hys, hyr, hes, her, hzs, hzr, halo_sem,
    vhx, vys, vyr, vzs, vzr, velocity_sem,
    msg, rxz, ry, sum_sem,
    sendp, recvp, sendv, recvv, particle_sem, vhi, vlo,
    send_sem, measure,
):
    gx, gy, gz = lax.axis_index("gx"), lax.axis_index("gy"), lax.axis_index("gz")

    def at_x(k):
        return (lax.rem(gx + (k + GX), GX), gy, gz)

    def at_y(k):
        return (gx, lax.rem(gy + (k + GY), GY), gz)

    def at_z(k):
        return (gx, gy, lax.rem(gz + (k + GZ), GZ))

    def near(d):
        return (
            lax.rem(gx + (d[0] + GX), GX),
            lax.rem(gy + (d[1] + GY), GY),
            lax.rem(gz + (d[2] + GZ), GZ),
        )

    barrier = pltpu.get_barrier_semaphore()
    for d in DIRECTIONS:
        pl.semaphore_signal(barrier, inc=1, device_id=near(d), device_id_type=MESH)
    for k in RING_Y:
        pl.semaphore_signal(barrier, inc=1, device_id=at_y(k), device_id_type=MESH)

    loads = {}
    for i, (name, source, target) in enumerate((
        ("src", src_in, src), ("vel", vel_in, vel), ("ky", ky_in, ky), ("kyt", kyt_in, kyt),
        ("met", met_in, met), ("scr", scr_in, scr), ("coords", coords_in, coords),
        ("owner", owner_in, owner), ("elem", elem_in, elem), ("lsc", lsc_in, lsc),
    )):
        loads[name] = pltpu.make_async_copy(source, target, load_sem.at[i])
        loads[name].start()

    sent_rows = []

    def remote(source, target, sem, device, rows):
        pltpu.make_async_remote_copy(
            src_ref=source,
            dst_ref=target,
            send_sem=send_sem.at[0],
            recv_sem=sem,
            device_id=device,
            device_id_type=MESH,
        ).start()
        sent_rows.append(rows)

    def wait_rows(sem, rows):
        piece = measure.at[pl.ds(0, rows)]
        pltpu.make_async_copy(piece, piece, sem).wait()

    row_id = iota((128, 128), 0)
    lane_id = iota((128, 128), 1)
    eye = row_id == lane_id
    lane_in = lane_id % 8
    low_z = (lane_in == 0) & (lane_id > 0)
    high_z = (lane_in == 7) & (lane_id < 127)
    at_floor = gy == 0
    at_ceiling = gy == GY - 1

    def source_mask():
        index = iota((16, 128), 0)
        lane = iota((16, 128), 1)
        from_x, from_y = index // 3 - 1, index % 3 - 1
        in_x, in_y = lane // 16, lane % 16
        keep = (index < 9) & jnp.logical_not((from_y == -1) & at_floor)
        keep = keep & jnp.logical_not((from_y == 1) & at_ceiling)
        keep = keep & ((from_x == 0) | ((from_x == -1) & (in_x == 0)) | ((from_x == 1) & (in_x == 7)))
        return keep & ((from_y == 0) | ((from_y == -1) & (in_y == 0)) | ((from_y == 1) & (in_y == 15)))

    z_keep = source_mask()

    in_y = lax.broadcasted_iota(jnp.int32, (2, 128), 1) % 16

    def pack_planes(f, field):
        pair = jnp.concatenate(
            [
                jnp.sum(jnp.where(eye, field[:, 127:128], 0.0), axis=0, keepdims=True),
                jnp.sum(jnp.where(eye, field[:, 0:1], 0.0), axis=0, keepdims=True),
            ],
            axis=0,
        )
        pair = (
            pair
            + jnp.where(in_y == 7, pltpu.roll(pair, 127, 1), 0.0)
            + jnp.where(in_y == 8, pltpu.roll(pair, 1, 1), 0.0)
        )
        for dx in (-1, 0, 1):
            for dy in (-1, 0, 1):
                shift = (16 * dx - 15 * dy) % 128
                hzs[f, (1 - dx) * 3 + (1 - dy)] = pltpu.roll(pair, shift, 1) if shift else pair

    def pack_faces(f, field):
        w = work.at[f]
        field = (
            field
            + jnp.where(low_z, pltpu.roll(field, 1, 1), 0.0)
            + jnp.where(high_z, pltpu.roll(field, 127, 1), 0.0)
        )
        w[...] = field
        both = w[pl.ds(7, 8, stride=16), :] + w[pl.ds(8, 8, stride=16), :]
        w[pl.ds(7, 8, stride=16), :] = both
        w[pl.ds(8, 8, stride=16), :] = both
        for d in DIRECTIONS:
            if d[2] == 0 and d[0] and d[1]:
                row = (112 if d[0] == 1 else 0) + (15 if d[1] == 1 else 0)
                hes[f, (1 - d[0]) + (1 - d[1]) // 2] = field[row : row + 1, :]
        hxs[f, 0] = w[pl.ds(112, 16), :]
        hxs[f, 1] = w[pl.ds(0, 16), :]
        hys[f, 0] = w[pl.ds(15, 8, stride=16), :]
        hys[f, 1] = w[pl.ds(0, 8, stride=16), :]

    def send_halo(f, planes):
        for d in DIRECTIONS:
            if planes != (d[2] != 0):
                continue
            rows = 1
            if d[2]:
                j, side = (1 - d[0]) * 3 + (1 - d[1]), (1 - d[2]) // 2
                source, target = hzs.at[f, j, pl.ds(side, 1)], hzr.at[f, side, pl.ds(j, 1)]
            elif d[0] and d[1]:
                e = (1 - d[0]) + (1 - d[1]) // 2
                source, target = hes.at[f, e], her.at[f, e]
            elif d[0]:
                source, target = hxs.at[f, (1 - d[0]) // 2], hx.at[f, (1 - d[0]) // 2]
                rows = 16
            else:
                source, target = hys.at[f, (1 - d[1]) // 2], hyr.at[f, (1 - d[1]) // 2]
                rows = 8
            remote(source, target, halo_sem.at[f, 1 if planes else 0], near(d), rows)

    def start_halo(f, field):
        pack_planes(f, field)
        send_halo(f, True)
        pack_faces(f, field)
        send_halo(f, False)

    def end_halo(f):
        w = work.at[f]
        wait_rows(halo_sem.at[f, 0], 52)
        w[pl.ds(0, 8, stride=16), :] = w[pl.ds(0, 8, stride=16), :] + jnp.where(at_floor, 0.0, hyr[f, 0])
        w[pl.ds(15, 8, stride=16), :] = w[pl.ds(15, 8, stride=16), :] + jnp.where(at_ceiling, 0.0, hyr[f, 1])
        w[pl.ds(0, 16), :] = w[pl.ds(0, 16), :] + hx[f, 0]
        w[pl.ds(112, 16), :] = w[pl.ds(112, 16), :] + hx[f, 1]
        for d in DIRECTIONS:
            if d[2] == 0 and d[0] and d[1]:
                e = (1 - d[0]) + (1 - d[1]) // 2
                row = (0 if d[0] == 1 else 112) + (0 if d[1] == 1 else 15)
                cut = at_floor if d[1] == 1 else at_ceiling
                w[pl.ds(row, 1), :] = w[pl.ds(row, 1), :] + jnp.where(cut, 0.0, her[f, e])
        field = w[...]
        wait_rows(halo_sem.at[f, 1], 18)
        low = jnp.sum(jnp.where(z_keep, hzr[f, 0], 0.0), axis=0, keepdims=True)
        high = jnp.sum(jnp.where(z_keep, hzr[f, 1], 0.0), axis=0, keepdims=True)
        low = jnp.sum(jnp.where(eye, low, 0.0), axis=1, keepdims=True)
        high = jnp.sum(jnp.where(eye, high, 0.0), axis=1, keepdims=True)
        return field + jnp.where(lane_id == 0, low, 0.0) + jnp.where(lane_id == 127, high, 0.0)

    def start_x():
        for c in range(3):
            remote(vel.at[c, pl.ds(112, 16)], vhx.at[c, 0], velocity_sem.at[0], at_x(1), 16)
            remote(vel.at[c, pl.ds(0, 16)], vhx.at[c, 1], velocity_sem.at[0], at_x(-1), 16)

    def mid_xy():
        wait_rows(velocity_sem.at[0], 96)
        for c in range(3):
            w = work.at[3 + c]
            w[...] = vel[c]
            w[pl.ds(0, 16), :] = w[pl.ds(0, 16), :] + vhx[c, 0]
            w[pl.ds(112, 16), :] = w[pl.ds(112, 16), :] + vhx[c, 1]
            both = w[pl.ds(7, 8, stride=16), :] + w[pl.ds(8, 8, stride=16), :]
            w[pl.ds(7, 8, stride=16), :] = both
            w[pl.ds(8, 8, stride=16), :] = both
            vys[c, 0] = w[pl.ds(15, 8, stride=16), :]
            vys[c, 1] = w[pl.ds(0, 8, stride=16), :]
            remote(vys.at[c, 0], vyr.at[c, 0], velocity_sem.at[1], at_y(1), 8)
            remote(vys.at[c, 1], vyr.at[c, 1], velocity_sem.at[1], at_y(-1), 8)

    def mid_yz():
        wait_rows(velocity_sem.at[1], 48)
        for c in range(3):
            w = work.at[3 + c]
            w[pl.ds(0, 8, stride=16), :] = w[pl.ds(0, 8, stride=16), :] + jnp.where(at_floor, 0.0, vyr[c, 0])
            w[pl.ds(15, 8, stride=16), :] = w[pl.ds(15, 8, stride=16), :] + jnp.where(at_ceiling, 0.0, vyr[c, 1])
            field = w[...]
            vzs[c, 0] = jnp.sum(jnp.where(eye, field[:, 127:128], 0.0), axis=0, keepdims=True)
            vzs[c, 1] = jnp.sum(jnp.where(eye, field[:, 0:1], 0.0), axis=0, keepdims=True)
            remote(vzs.at[c, 0], vzr.at[c, 0], velocity_sem.at[2], at_z(1), 1)
            remote(vzs.at[c, 1], vzr.at[c, 1], velocity_sem.at[2], at_z(-1), 1)
            w[...] = (
                field
                + jnp.where(low_z, pltpu.roll(field, 1, 1), 0.0)
                + jnp.where(high_z, pltpu.roll(field, 127, 1), 0.0)
            )

    def end_z():
        wait_rows(velocity_sem.at[2], 6)
        for c in range(3):
            field = work[3 + c]
            low = jnp.sum(jnp.where(eye, vzr[c, 0], 0.0), axis=1, keepdims=True)
            high = jnp.sum(jnp.where(eye, vzr[c, 1], 0.0), axis=1, keepdims=True)
            field = field + jnp.where(lane_id == 0, low, 0.0) + jnp.where(lane_id == 127, high, 0.0)
            high = field.astype(BF16)
            vhi[pl.ds(128 * c, 128), :] = high
            vlo[pl.ds(128 * c, 128), :] = (field - high.astype(F32)).astype(BF16)

    table = deriv_table()

    def along_x(field, transposed):
        parts = [field[16 * i : 16 * i + 16, :] for i in range(8)]
        out = []
        for a in range(8):
            total = None
            for i in range(8):
                factor = table[i][a] if transposed else table[a][i]
                if factor == 0.0:
                    continue
                term = parts[i] * np.float32(factor)
                total = term if total is None else total + term
            out.append(total)
        return jnp.concatenate(out, axis=0)

    def gradients(field):
        return (
            along_x(field, False),
            jnp.dot(ky[...], field, precision=EXACT, preferred_element_type=F32),
            jnp.dot(field, kyt[...], precision=EXACT, preferred_element_type=F32),
        )

    def operator(field):
        dx, dy, dz = gradients(field)
        return (
            along_x(met[0] * dx, True)
            + jnp.dot(kyt[...], met[1] * dy, precision=EXACT, preferred_element_type=F32)
            + jnp.dot(met[2] * dz, ky[...], precision=EXACT, preferred_element_type=F32)
            + scr[...] * field
        ) * SCALE

    sendv[...] = jnp.zeros_like(sendv)
    loads["src"].wait()
    pack_planes(0, src[...])
    pack_faces(0, src[...])
    pl.semaphore_wait(barrier, len(DIRECTIONS) + len(RING_Y))
    send_halo(0, True)
    send_halo(0, False)
    loads["vel"].wait()
    start_x()

    loads["coords"].wait()
    loads["owner"].wait()
    loads["elem"].wait()
    owned = (owner[...] == iota((GY, 512), 0)).astype(F32)
    tri = (iota((128, 128), 0) < iota((128, 128), 1)).astype(BF16)
    before = jnp.zeros((GY, 1), F32)
    rank = []
    for b in range(4):
        part = owned[:, 128 * b : 128 * b + 128]
        count = jnp.dot(part.astype(BF16), tri, preferred_element_type=F32) + before
        rank.append(jnp.sum(count * part, axis=0, keepdims=True))
        before = before + jnp.sum(part, axis=1, keepdims=True)
    rank = jnp.concatenate(rank, axis=1)
    slots = (rank.astype(jnp.int32) == iota((CAP, 512), 0)).astype(F32)
    data = jnp.concatenate(
        [coords[...], elem[...].astype(F32), jnp.zeros((4, 512), F32)], axis=0
    )
    lhs = jnp.concatenate([data * owned[g : g + 1, :] for g in range(GY)], axis=0)
    packed = lax.dot_general(
        lhs, slots, (((1,), (1,)), ((), ())), precision=EXACT, preferred_element_type=F32
    )
    for g in range(GY):
        sendp[g] = packed[8 * g : 8 * g + 8, :]

    for k in range(1, GY):
        peer = lax.rem(gy + k, GY)
        remote(sendp.at[peer], recvp.at[gy], particle_sem.at[0], (gx, peer, gz), 8)
    recvp[gy] = sendp[gy]

    mid_xy()
    loads["ky"].wait()
    loads["kyt"].wait()
    loads["met"].wait()
    loads["scr"].wait()
    v0 = end_halo(0)

    image0 = operator(v0)
    start_halo(1, image0)
    mid_yz()
    v1 = end_halo(1)
    image1 = operator(v1)
    start_halo(2, image1)
    place_y = row_id % 16
    share_x = jnp.where((row_id < 16) | (row_id >= 112), 0.5, 1.0)
    edge_y = (place_y % 8 == 0) | (place_y % 8 == 7)
    wall = ((place_y == 0) & at_floor) | ((place_y == 15) & at_ceiling)
    share_y = jnp.where(edge_y & jnp.logical_not(wall), 0.5, 1.0)
    share_z = jnp.where((lane_in == 0) | (lane_in == 7), 0.5, 1.0)
    weight = share_x * share_y * share_z
    early = jnp.concatenate(
        [
            jnp.sum(value, axis=0, keepdims=True)
            for value in (weight * v0 * v0, v0 * image0, weight * v1 * v1, v1 * image1)
        ],
        axis=0,
    )
    end_z()

    loads["lsc"].wait()
    wait_rows(particle_sem.at[0], 8 * (GY - 1))
    points = gll_points()
    node = iota((8, 128), 0)

    def basis(coord):
        product = lsc[...]
        for m in range(8):
            product = product * jnp.where(node == m, 1.0, coord - np.float32(points[m]))
        return product

    def sample_two(step, carry):
        low_parts, high_parts, weights = [], [], []
        for half in range(2):
            block = recvp[2 * step + half]
            element = block[3:4, :].astype(jnp.int32)
            bx, by, bz = (basis(block[d : d + 1, :]) for d in range(3))
            element_y = element // 16
            element_z = element % 16
            wide = jnp.concatenate(
                [jnp.where(element_z == e, bz, 0.0) for e in range(16)], axis=0
            )
            high = wide.astype(BF16)
            high_parts.append(high)
            low_parts.append((wide - high.astype(F32)).astype(BF16))
            tall = jnp.concatenate(
                [jnp.where(element_y == e, by, 0.0) for e in range(2)], axis=0
            )
            weights.append(
                jnp.concatenate([bx[i : i + 1, :] * tall for i in range(8)], axis=0)
            )
        high = jnp.concatenate(high_parts, axis=1)
        low = jnp.concatenate(low_parts, axis=1)
        for c in range(3):
            vh = vhi[pl.ds(128 * c, 128), :]
            partial = (
                jnp.dot(vh, high, preferred_element_type=F32)
                + jnp.dot(vh, low, preferred_element_type=F32)
                + jnp.dot(vlo[pl.ds(128 * c, 128), :], high, preferred_element_type=F32)
            )
            for half in range(2):
                sendv[2 * step + half, pl.ds(c, 1), :] = jnp.sum(
                    partial[:, 128 * half : 128 * half + 128] * weights[half], axis=0, keepdims=True
                )
        return carry

    lax.fori_loop(0, GY // 2, sample_two, 0)

    for k in range(1, GY):
        peer = lax.rem(gy + k, GY)
        remote(sendv.at[peer], recvv.at[gy], particle_sem.at[1], (gx, peer, gz), 8)
    recvv[gy] = sendv[gy]
    v2 = end_halo(2)

    dx, dy, dz = gradients(v2)
    rows = jnp.concatenate(
        [
            early,
            jnp.sum(weight * v2 * v2, axis=0, keepdims=True),
            jnp.sum(
                (met[0] * dx * dx + met[1] * dy * dy + met[2] * dz * dz + scr[...] * v2 * v2) * SCALE,
                axis=0,
                keepdims=True,
            ),
            jnp.zeros((2, 128), F32),
        ],
        axis=0,
    )
    total = jnp.sum(rows, axis=1, keepdims=True)
    row = jnp.sum(
        jnp.where(iota((8, 128), 0) == iota((8, 128), 1), total, 0.0), axis=0, keepdims=True
    )

    msg[0] = row
    here = gx * GZ + gz
    rxz[here] = row
    for i, k in FAR_XZ:
        device = (lax.rem(gx + i, GX), gy, lax.rem(gz + k, GZ))
        remote(msg.at[0], rxz.at[here], sum_sem.at[0], device, 1)
    wait_rows(sum_sem.at[0], GX * GZ - 1)
    row = tree([rxz[k] for k in range(GX * GZ)])
    msg[1] = row
    ry[gy] = row
    for k in FAR_Y:
        remote(msg.at[1], ry.at[gy], sum_sem.at[1], at_y(k), 1)

    wait_rows(particle_sem.at[1], 8 * (GY - 1))
    back = jnp.concatenate([recvv[g] for g in range(GY)], axis=0)
    spread = jnp.dot(back, slots, precision=EXACT, preferred_element_type=F32)
    velocity = jnp.zeros((8, 512), F32)
    for g in range(GY):
        velocity = velocity + spread[8 * g : 8 * g + 8, :] * owned[g : g + 1, :]
    pv_out[...] = velocity[0:3, :]

    wait_rows(sum_sem.at[1], GY - 1)
    row = tree([ry[k] for k in range(GY)])

    lane = iota((1, 128), 1)
    m = [jnp.sum(jnp.where(lane == k, row, 0.0), axis=1, keepdims=True) for k in range(6)]

    def form(coefficients, shift):
        total = None
        for i, left in enumerate(coefficients):
            for j, right in enumerate(coefficients):
                term = left * right * m[i + j + shift]
                total = term if total is None else total + term
        return total

    one = jnp.ones_like(m[0])
    rr = m[0]
    direction = [one]
    residual = [one]
    solution_row = [jnp.zeros_like(one)] * 3
    for step in range(3):
        alpha = rr / form(direction, 1)
        for i, value in enumerate(direction):
            solution_row[i] = solution_row[i] + alpha * value
        if step == 2:
            break
        residual = residual + [jnp.zeros_like(one)]
        for i, value in enumerate(direction):
            residual[i + 1] = residual[i + 1] - alpha * value
        new = form(residual, 0)
        beta = new / rr
        direction = [
            value + beta * direction[i] if i < len(direction) else value
            for i, value in enumerate(residual)
        ]
        rr = new
    p_out[...] = (solution_row[0] * v0 + solution_row[1] * v1 + solution_row[2] * v2) * SCALE

    wait_rows(send_sem.at[0], sum(sent_rows))
    assert sum(sent_rows) == SENT_ROWS


def write_out(p_in, pv_in, p_out, pv_out, sem):
    copies = [
        pltpu.make_async_copy(p_in, p_out, sem.at[0]),
        pltpu.make_async_copy(pv_in, pv_out, sem.at[1]),
    ]
    for copy in copies:
        copy.start()
    for copy in copies:
        copy.wait()


def body(vel, src, met, scr, coords, owner, elem):
    table = np.array(deriv_table(), np.float32)
    kron = np.kron(np.eye(16, dtype=np.float32), table)
    lsc = np.repeat(np.array(lagrange_scale(), np.float32)[:, None], 128, axis=1)
    operands = (
        vel.reshape(3, 128, 128),
        src.reshape(128, 128),
        met.reshape(3, 128, 128),
        scr.reshape(128, 128),
        coords,
        owner.reshape(1, 512),
        elem.reshape(1, 512),
        jnp.asarray(kron),
        jnp.asarray(kron.T),
        jnp.asarray(lsc),
    )
    anywhere = pl.BlockSpec(memory_space=pl.ANY)
    vmem = pl.BlockSpec(memory_space=pltpu.VMEM)
    dma = pltpu.SemaphoreType.DMA
    pressure, velocity = pl.pallas_call(
        kernel,
        out_shape=(
            pltpu.VMEM((128, 128), F32),
            pltpu.VMEM((3, 512), F32),
        ),
        in_specs=[anywhere] * len(operands),
        out_specs=(vmem, vmem),
        scratch_shapes=[pltpu.VMEM(x.shape, x.dtype) for x in operands]
        + [
            dma((len(operands),)),
            pltpu.VMEM((6, 128, 128), F32),
            pltpu.VMEM((3, 2, 16, 128), F32),
            pltpu.VMEM((3, 2, 16, 128), F32),
            pltpu.VMEM((3, 2, 8, 128), F32),
            pltpu.VMEM((3, 2, 8, 128), F32),
            pltpu.VMEM((3, 4, 1, 128), F32),
            pltpu.VMEM((3, 4, 1, 128), F32),
            pltpu.VMEM((3, 9, 2, 128), F32),
            pltpu.VMEM((3, 2, 16, 128), F32),
            dma((3, 2)),
            pltpu.VMEM((3, 2, 16, 128), F32),
            pltpu.VMEM((3, 2, 8, 128), F32),
            pltpu.VMEM((3, 2, 8, 128), F32),
            pltpu.VMEM((3, 2, 1, 128), F32),
            pltpu.VMEM((3, 2, 1, 128), F32),
            dma((3,)),
            pltpu.VMEM((2, 1, 128), F32),
            pltpu.VMEM((GX * GZ, 1, 128), F32),
            pltpu.VMEM((GY, 1, 128), F32),
            dma((2,)),
            pltpu.VMEM((GY, 8, 128), F32),
            pltpu.VMEM((GY, 8, 128), F32),
            pltpu.VMEM((GY, 8, 128), F32),
            pltpu.VMEM((GY, 8, 128), F32),
            dma((2,)),
            pltpu.VMEM((384, 128), BF16),
            pltpu.VMEM((384, 128), BF16),
            dma((1,)),
            pltpu.VMEM((SENT_ROWS, 1, 128), F32),
        ],
        compiler_params=pltpu.CompilerParams(collective_id=0, has_side_effects=True),
        name="step",
    )(*operands)
    pressure = pltpu.with_memory_space_constraint(pressure, pltpu.VMEM)
    velocity = pltpu.with_memory_space_constraint(velocity, pltpu.VMEM)
    pressure, velocity = pl.pallas_call(
        write_out,
        out_shape=(
            jax.ShapeDtypeStruct((128, 128), F32),
            jax.ShapeDtypeStruct((3, 512), F32),
        ),
        in_specs=[vmem, vmem],
        out_specs=(anywhere, anywhere),
        scratch_shapes=[dma((2,))],
        name="write_out",
    )(pressure, velocity)
    return pressure.reshape(8, 16, 128), velocity


def solution(mesh):
    in_specs = (
        P(None, "gx", "gy", "gz"),
        P("gx", "gy", "gz"),
        P(None, "gx", "gy", "gz"),
        P("gx", "gy", "gz"),
        P(None, ("gx", "gy", "gz")),
        P(("gx", "gy", "gz"), None),
        P(("gx", "gy", "gz")),
    )
    out_specs = (P("gx", "gy", "gz"), P(None, ("gx", "gy", "gz")))
    return jax.shard_map(body, mesh=mesh, in_specs=in_specs, out_specs=out_specs, check_vma=False)
```
